32 devices in a mesh: shard: 2 (over x), ctx: 4 (over z), tp: 4 (over y, core).
Axes of the slice: x: 2, y: 2, z: 4, core: 2. Of those that a mesh axis runs over, the one named last changes fastest.
Arguments:
- frames: bfloat16 [2, 2, 2048, 1280], P(None, 'shard', 'ctx'), may hold values from -6 to 6
- lengths: int32 [2, 2], P(None, 'shard'), may hold values from 0 to 2048, as said below
- first_gain: bfloat16 [1280], replicated, may hold values from 0.25 to 1.75
- first_bias: bfloat16 [1280], replicated, may hold values from -3 to 3
- query_weight: bfloat16 [1280, 1280], P('shard', 'tp'), may hold values from -0.15625 to 0.15625
- query_bias: bfloat16 [1280], P('tp'), may hold values from -3 to 3
- key_weight: bfloat16 [1280, 1280], P('shard', 'tp'), may hold values from -0.15625 to 0.15625
- value_weight: bfloat16 [1280, 1280], P('shard', 'tp'), may hold values from -0.15625 to 0.15625
- value_bias: bfloat16 [1280], P('tp'), may hold values from -0.088378906 to 0.088378906
- output_weight: bfloat16 [1280, 1280], P('shard', 'tp'), may hold values from -4 to 4
- output_bias: bfloat16 [1280], replicated, may hold values from -3 to 3
- second_gain: bfloat16 [1280], replicated, may hold values from 0.25 to 1.75
- second_bias: bfloat16 [1280], replicated, may hold values from -3 to 3
- inner_weight: bfloat16 [1280, 5120], P('shard', 'tp'), may hold values from -0.15625 to 0.15625
- inner_bias: bfloat16 [5120], P('tp'), may hold values from -3 to 3
- outer_weight: bfloat16 [1280, 5120], P('shard', 'tp'), may hold values from -0.15625 to 0.15625
- outer_bias: bfloat16 [1280], replicated, may hold values from -3 to 3
- cotangent: bfloat16 [2, 2, 2048, 1280], P(None, 'shard', 'ctx'), may hold values from -6 to 6
Outputs:
- result: bfloat16 [2, 2, 2048, 1280], P(None, 'shard', 'ctx')
- frames_grad: bfloat16 [2, 2, 2048, 1280], P(None, 'shard', 'ctx')
- first_gain_grad: float32 [1280], replicated
- first_bias_grad: float32 [1280], replicated
- query_weight_grad: float32 [1280, 1280], P('shard', 'tp')
- query_bias_grad: float32 [1280], P('tp')
- key_weight_grad: float32 [1280, 1280], P('shard', 'tp')
- value_weight_grad: float32 [1280, 1280], P('shard', 'tp')
- value_bias_grad: float32 [1280], P('tp')
- output_weight_grad: float32 [1280, 1280], P('shard', 'tp')
- output_bias_grad: float32 [1280], replicated
- second_gain_grad: float32 [1280], replicated
- second_bias_grad: float32 [1280], replicated
- inner_weight_grad: float32 [1280, 5120], P('shard', 'tp')
- inner_bias_grad: float32 [5120], P('tp')
- outer_weight_grad: float32 [1280, 5120], P('shard', 'tp')
- outer_bias_grad: float32 [1280], replicated
The draws below stay inside these ranges and needn't reach their ends.
Inputs may be any that keep to these rules, and one draw needn't show every extreme that they name: Slot lengths count a clip's first frames; 0 marks an empty slot; in every draw some slot is empty and some slot is full.
All inputs are finite; a program needn't handle non-finite values.
Results may differ from the reference program's by a relative error of at most 0.025.
Values may be sent and summed in bfloat16 or wider, within the bound.
No kernel may reach another device: no remote copies, remote signals or barrier semaphores. Data moves between devices by JAX's collectives and lax.ppermute only.
A program may use at most 192 MiB of HBM per device.

```python
import math
import jax
import jax.numpy as jnp
from jax import lax

D = 1280
H = 16
HD = 80
FF = 5120
MICRO = 2
SLOT = 2048
CLIPS_MB = 2
N_TP = 4


def draw_lengths(key, part):
    first_key, second_key = jax.random.split(key)
    slot_count = MICRO * CLIPS_MB
    drawn_lengths = jax.random.randint(first_key, (slot_count,), SLOT // 8, SLOT + 1)
    shuffled = jax.random.permutation(second_key, slot_count)
    drawn_lengths = drawn_lengths.at[shuffled[0]].set(SLOT).at[shuffled[1]].set(0)
    return drawn_lengths.reshape(MICRO, CLIPS_MB).astype(jnp.int32)


def level_of(own_key, shape, cuts, low, top_value):
    def one(dim, blocks):
        steps = jax.random.uniform(jax.random.fold_in(jax.random.fold_in(own_key, 6), dim), (blocks,), jnp.float32, low / len(cuts), top_value / len(cuts))
        return jnp.repeat(jnp.exp(steps), shape[dim] // blocks).reshape((-1,) + (1,) * (len(shape) - dim - 1))

    factor_of = one(*cuts[0])
    for cut in cuts[1:]:
        factor_of = factor_of * one(*cut)
    return factor_of


def scatter_about(own_key, shape, scale, most, pieces=(), held_as=jnp.bfloat16):
    drawn = scale * jax.random.normal(own_key, shape, jnp.float32)
    if pieces:
        drawn = drawn * level_of(own_key, shape, pieces, -0.22, 0.18)
    return jnp.clip(drawn, -most, most).astype(held_as)


def setup_inputs(seed: int = 0) -> dict:
    key_list = jax.random.split(jax.random.key(seed), 19)
    return {
        "frames": scatter_about(key_list[0], (MICRO, CLIPS_MB, SLOT, D), 1.0, 6.0, ((1, 2), (2, 4))),
        "lengths": draw_lengths(jax.random.fold_in(key_list[18], 71), 0),
        "first_gain": jnp.clip(1.0 + 0.15 * jax.random.normal(key_list[2], (D,), jnp.float32), 0.25, 1.75).astype(jnp.bfloat16),
        "first_bias": scatter_about(key_list[3], (D,), 0.3, 3.0),
        "query_weight": scatter_about(key_list[4], (D, D), D ** -0.5, 0.15625, ((0, 2), (1, 4))),
        "query_bias": scatter_about(key_list[5], (D,), 0.3, 3.0, ((0, 4),)),
        "key_weight": scatter_about(key_list[6], (D, D), D ** -0.5, 0.15625, ((0, 2), (1, 4))),
        "value_weight": scatter_about(key_list[7], (D, D), D ** -0.5, 0.15625, ((0, 2), (1, 4))),
        "value_bias": scatter_about(key_list[8], (D,), (1.0 / SLOT ** 0.5), 0.088378906, ((0, 4),)),
        "output_weight": scatter_about(key_list[9], (D, D), (max(1, 4 * D // SLOT)) ** -0.5, 4.0, ((0, 2), (1, 4))),
        "output_bias": scatter_about(key_list[10], (D,), 0.3, 3.0),
        "second_gain": jnp.clip(1.0 + 0.15 * jax.random.normal(key_list[11], (D,), jnp.float32), 0.25, 1.75).astype(jnp.bfloat16),
        "second_bias": scatter_about(key_list[12], (D,), 0.3, 3.0),
        "inner_weight": scatter_about(key_list[13], (D, FF), D ** -0.5, 0.15625, ((0, 2), (1, 4))),
        "inner_bias": scatter_about(key_list[14], (FF,), 0.5, 3.0, ((0, 4),)),
        "outer_weight": scatter_about(key_list[15], (D, FF), (FF // 4) ** -0.5, 0.15625, ((0, 2), (1, 4))),
        "outer_bias": scatter_about(key_list[16], (D,), 0.3, 3.0),
        "cotangent": scatter_about(key_list[17], (MICRO, CLIPS_MB, SLOT, D), 1.0, 6.0, ((1, 2), (2, 4))),
    }


epsilon = 1e-05
highest = lax.Precision.HIGHEST

@jax.custom_vjp
def low(v):
    return lax.optimization_barrier(v.astype(jnp.bfloat16)).astype(jnp.float32)

@jax.custom_vjp
def low_back(v):
    return v

def low_keep(v):
    return (low(v), None)

def low_pass(kept, grad):
    return (grad,)

def back_keep(v):
    return (v, None)

def back_low(kept, grad):
    return (low(grad),)
low.defvjp(low_keep, low_pass)
low_back.defvjp(back_keep, back_low)

def layer_norm(values, scale_gain, shift_bias):
    center = values - lax.optimization_barrier(jnp.mean(values, -1, keepdims=True))
    spread = lax.optimization_barrier(jnp.mean(center * center, -1, keepdims=True))
    return center * lax.rsqrt(spread + epsilon) * scale_gain + shift_bias

def attend_block(query_block, key_rows, value_rows, key_valid, has_frames):
    scores = low_back(jnp.einsum('hqd,hkd->hqk', query_block, key_rows, precision=highest)) * (1.0 / math.sqrt(HD))
    expo = jnp.where(key_valid[None, None, :], jnp.exp(scores), 0.0)
    weight_total = lax.optimization_barrier(jnp.sum(expo, -1))
    unnormal = low_back(jnp.einsum('hqk,hkd->hqd', low(expo), value_rows, precision=highest))
    return unnormal / jnp.where(has_frames, weight_total, 1.0)[:, :, None]

def heads_first(array):
    return array.reshape(N_TP, SLOT, H // N_TP, HD).transpose(0, 2, 1, 3).reshape(H, SLOT, HD)

def heads_back(array):
    return array.reshape(N_TP, H // N_TP, SLOT, HD).transpose(0, 2, 1, 3).reshape(N_TP, SLOT, D // N_TP)

def clip_forward(params, clip_frames, length):
    first_gain, first_bias, query_weight, query_bias, key_weight, value_weight, value_bias, output_weight, output_bias, second_gain, second_bias, inner_weight, inner_bias, outer_weight, outer_bias = params
    group_width = D // N_TP
    hidden = FF // N_TP
    frame_valid = jnp.arange(SLOT) < length
    has_frames = length > 0
    normed = low(layer_norm(clip_frames, first_gain, first_bias))
    copies = low_back(jnp.broadcast_to(normed, (N_TP, SLOT, D)))

    def project(weight):
        return jnp.einsum('gsd,dgc->gsc', copies, weight.reshape(D, N_TP, group_width), precision=highest)
    queries = low_back(low(project(query_weight) + query_bias.reshape(N_TP, 1, group_width)))
    key_rows = low_back(low(project(key_weight)))
    value_rows = low_back(low(project(value_weight) + value_bias.reshape(N_TP, 1, group_width)))
    block_rows = min(512, SLOT)
    query_blocks = heads_first(queries).reshape(H, SLOT // block_rows, block_rows, HD).transpose(1, 0, 2, 3)
    key_heads = heads_first(key_rows)
    value_heads = heads_first(value_rows)
    attend = jax.checkpoint(lambda query_block: attend_block(query_block, key_heads, value_heads, frame_valid, has_frames))
    attended = lax.map(attend, query_blocks).transpose(1, 0, 2, 3).reshape(H, SLOT, HD)
    mixed_heads = low(heads_back(attended))
    partial_out = low(jnp.einsum('gsc,egc->gse', mixed_heads, output_weight.reshape(D, N_TP, group_width), precision=highest))
    middle = clip_frames + low_back(lax.optimization_barrier(jnp.sum(partial_out, 0))) + output_bias
    normed_two = low(layer_norm(middle, second_gain, second_bias))
    copies_two = low_back(jnp.broadcast_to(normed_two, (N_TP, SLOT, D)))
    inner_linear = low_back(jnp.einsum('gsd,dgf->gsf', copies_two, inner_weight.reshape(D, N_TP, hidden), precision=highest))
    inner_linear = inner_linear + inner_bias.reshape(N_TP, 1, hidden)
    activated = low(jax.nn.gelu(inner_linear, approximate=False))
    partial_ffn = low(jnp.einsum('gsf,egf->gse', activated, outer_weight.reshape(D, N_TP, hidden), precision=highest))
    return middle + low_back(lax.optimization_barrier(jnp.sum(partial_ffn, 0))) + outer_bias

def reference(frames, lengths, first_gain, first_bias, query_weight, query_bias, key_weight, value_weight, value_bias, output_weight, output_bias, second_gain, second_bias, inner_weight, inner_bias, outer_weight, outer_bias, cotangent):
    params = tuple((member.astype(jnp.float32) for member in (first_gain, first_bias, query_weight, query_bias, key_weight, value_weight, value_bias, output_weight, output_bias, second_gain, second_bias, inner_weight, inner_bias, outer_weight, outer_bias)))
    full_shape = frames.shape
    clips = frames.astype(jnp.float32).reshape(MICRO * CLIPS_MB, SLOT, D)
    clip_lengths = lengths.reshape(MICRO * CLIPS_MB).astype(jnp.int32)

    def whole_layer(weights, inputs):
        return lax.map(lambda member: jax.checkpoint(clip_forward)(weights, member[0], member[1]), (inputs, clip_lengths))
    results, pullback = jax.vjp(whole_layer, params, clips)
    frame_mask = (jnp.arange(SLOT)[None, :] < clip_lengths[:, None]).astype(jnp.float32)
    seeds = cotangent.astype(jnp.float32).reshape(MICRO * CLIPS_MB, SLOT, D) * frame_mask[:, :, None]
    gradients, clip_grads = pullback(seeds)
    return (results.reshape(full_shape).astype(jnp.bfloat16), clip_grads.reshape(full_shape).astype(jnp.bfloat16), gradients[0], gradients[1], gradients[2], gradients[3], gradients[4], gradients[5], gradients[6], gradients[7], gradients[8], gradients[9], gradients[10], gradients[11], gradients[12], gradients[13], gradients[14])
```

```python
import functools
import math

import jax
import jax.numpy as jnp
from jax import lax
from jax.experimental import pallas as pl
from jax.experimental.pallas import tpu as pltpu
from jax.sharding import PartitionSpec as P

HD = 80
EXT = 96
EPS = 1e-05
BF = jnp.bfloat16
F32 = jnp.float32
SCALE = 1.0 / math.sqrt(HD)
SCALE2 = SCALE * math.log2(math.e)
SLOTS = (0, 2, 1, 3)
NT = (((1,), (1,)), ((), ()))
TN = (((0,), (0,)), ((), ()))


def sds(shape, kind):
    return jax.ShapeDtypeStruct(shape, kind)


def dot(left, right):
    return jnp.dot(left, right, preferred_element_type=F32)


def dot_nt(left, right):
    return lax.dot_general(left, right, NT, preferred_element_type=F32)


def dot_tn(left, right):
    return lax.dot_general(left, right, TN, preferred_element_type=F32)


def normalize(values):
    center = values - jnp.mean(values, -1, keepdims=True)
    spread = jnp.mean(center * center, -1, keepdims=True)
    inverse = lax.rsqrt(spread + EPS)
    return center * inverse, inverse


def norm_back(unit, inverse, grad, gain):
    scaled = grad * gain
    first = jnp.mean(scaled, -1, keepdims=True)
    second = jnp.mean(scaled * unit, -1, keepdims=True)
    return inverse * (scaled - first - unit * second)


SMEM = pl.BlockSpec(memory_space=pltpu.SMEM)


def front_kernel(micro, ids, fa, fb, ca, cb, gain, bias, normed_o, low_o):
    half = fa.shape[-1]
    rows = fa.shape[-2]
    piece = pl.program_id(0)
    va = fa[0].astype(F32)
    vb = fb[0].astype(F32)
    count = 2 * half
    mean = (jnp.sum(va, -1, keepdims=True) + jnp.sum(vb, -1, keepdims=True)) / count
    va = va - mean
    vb = vb - mean
    spread = (jnp.sum(va * va, -1, keepdims=True) + jnp.sum(vb * vb, -1, keepdims=True)) / count
    inverse = lax.rsqrt(spread + EPS)
    normed_o[:, :half] = (va * inverse * gain[:, :half] + bias[:, :half]).astype(BF)
    normed_o[:, half:] = (vb * inverse * gain[:, half:] + bias[:, half:]).astype(BF)
    start = ids[6] * (rows * 4) + ids[piece] * rows
    valid = start + lax.broadcasted_iota(jnp.int32, (rows, 1), 0) < ids[8 + micro]
    low_o[:, :half] = jnp.where(valid, ca[0].astype(F32), 0.0).astype(BF)
    low_o[:, half:] = jnp.where(valid, cb[0].astype(F32), 0.0).astype(BF)


def front(micro, ids, frames, cotangent, gain, bias):
    rows, width = frames.shape[1:]
    quarter = rows // 4
    half = width // 2
    own = pl.BlockSpec((1, quarter, half), lambda p, ids: (micro, ids[p], ids[4]))
    other = pl.BlockSpec((1, quarter, half), lambda p, ids: (micro, ids[p], ids[5]))
    line = pl.BlockSpec((1, width), lambda p, ids: (0, 0))
    out = pl.BlockSpec((quarter, width), lambda p, ids: (p, 0))
    return pl.pallas_call(
        functools.partial(front_kernel, micro),
        out_shape=(sds((rows, width), BF), sds((rows, width), BF)),
        grid_spec=pltpu.PrefetchScalarGridSpec(
            num_scalar_prefetch=1,
            grid=(4,),
            in_specs=[own, other, own, other, line, line],
            out_specs=[out, out],
        ),
        name="front",
    )(ids, frames, frames, cotangent, cotangent, gain, bias)


def heads_out(ids, store, offset, outs, count, step):
    for slot in range(len(outs)):
        begin = pl.multiple_of((ids[6] ^ slot) * HD, 16)
        outs[slot][offset : offset + HD, :] = store[pl.ds(begin, HD), :]


def project_kernel(ids, normed, qa, qb, ka, kb, va, vb, q_bias, v_bias, o0, o1, o2, o3, store):
    half = qa.shape[0]
    left = normed[:, :half]
    right = normed[:, half:]
    outs = (o0, o1, o2, o3)
    for order, (first, second, shift) in enumerate(
        ((qa, qb, q_bias), (ka, kb, None), (va, vb, v_bias))
    ):
        value = dot(left, first[...]) + dot(right, second[...])
        if shift is not None:
            value = value + shift[...]
        store[...] = value.T.astype(BF)
        heads_out(ids, store, order * HD, outs, 4, HD)


def project(ids, normed, weights, q_bias, v_bias):
    rows = normed.shape[0]
    width = weights[0].shape[1]
    return pl.pallas_call(
        project_kernel,
        out_shape=tuple(sds((3 * HD, rows), BF) for _ in range(4)),
        in_specs=[SMEM] + [pl.BlockSpec()] * 9,
        scratch_shapes=[pltpu.VMEM((width, rows), BF)],
        name="project",
    )(ids, normed, *weights, q_bias, v_bias)


def attend_kernel(plan, x0, x1, x2, x3, mask, o0, o1, o2, o3, kept, total, qs, ks, vs):
    rows = x0.shape[1]
    tail = EXT - HD
    first = lax.broadcasted_iota(jnp.int32, (tail, rows), 0) == 0
    ones = jnp.where(first, 1.0, 0.0).astype(BF)
    for slot, ref in enumerate((x0, x1, x2, x3)):
        qs[slot, :HD, :] = ref[:HD, :]
        qs[slot, HD:, :] = ones
        vs[slot, :HD, :] = ref[2 * HD :, :]
        vs[slot, HD:, :] = ones
        shift = jnp.where(first, mask[slot], 0.0)
        whole = jnp.concatenate([ref[HD : 2 * HD, :].astype(F32), shift], 0)
        ks[slot] = whole.T.astype(BF)
    has = plan[0] > 0

    def query_step(i, carry):
        query = qs[i]

        def key_step(n, acc):
            j = plan[1 + n]
            score = dot(ks[j], query)
            expo = jnp.exp2(score * SCALE2).astype(BF)
            return acc + dot(vs[j], expo)

        acc = lax.fori_loop(0, plan[0], key_step, jnp.zeros((EXT, rows), F32))
        denom = jnp.where(has, acc[HD : HD + 1, :], 1.0)
        attended = acc[:HD, :] / denom
        kept[i] = attended
        total[i] = denom
        return carry

    lax.fori_loop(0, 4, query_step, 0)
    for slot, ref in enumerate((o0, o1, o2, o3)):
        ref[...] = kept[slot].astype(BF)


def attend(plan, slabs, mask):
    rows = slabs[0].shape[1]
    return pl.pallas_call(
        attend_kernel,
        out_shape=tuple(sds((HD, rows), BF) for _ in range(4))
        + (sds((4, HD, rows), F32), sds((4, 1, rows), F32)),
        in_specs=[SMEM] + [pl.BlockSpec()] * 5,
        scratch_shapes=[
            pltpu.VMEM((4, EXT, rows), BF),
            pltpu.VMEM((4, rows, EXT), BF),
            pltpu.VMEM((4, EXT, rows), BF),
        ],
        name="attend",
    )(plan, *slabs, mask)


def attend_back_kernel(
    plan,
    x0,
    x1,
    x2,
    x3,
    g0,
    g1,
    g2,
    g3,
    kept,
    total,
    mask,
    o0,
    o1,
    o2,
    o3,
    qs,
    qt,
    ks,
    kt,
    vs,
    ss,
    st,
    deltas,
    gq,
    gk,
    gv,
):
    rows = x0.shape[1]
    tail = EXT - HD
    first = lax.broadcasted_iota(jnp.int32, (tail, rows), 0) == 0
    ones = jnp.where(first, 1.0, 0.0).astype(BF)
    blank = jnp.zeros((tail, rows), BF)
    blank_wide = jnp.zeros((tail, rows), F32)
    for slot, (ref, grad_ref) in enumerate(zip((x0, x1, x2, x3), (g0, g1, g2, g3))):
        qs[slot, :HD, :] = ref[:HD, :]
        qs[slot, HD:, :] = ones
        qt[slot] = jnp.concatenate([ref[:HD, :].astype(F32), blank_wide], 0).T.astype(BF)
        kt[slot] = ref[HD : 2 * HD, :]
        shift = jnp.where(first, mask[slot], 0.0)
        ks[slot] = jnp.concatenate([ref[HD : 2 * HD, :].astype(F32), shift], 0).T.astype(BF)
        vs[slot] = jnp.concatenate([ref[2 * HD :, :].astype(F32), blank_wide], 0).T.astype(BF)
        grad = grad_ref[...].astype(F32)
        recip = 1.0 / total[slot]
        deltas[slot] = jnp.sum(grad * kept[slot], 0, keepdims=True) * recip
        scaled = (grad * recip).astype(BF)
        ss[slot, :HD, :] = scaled
        ss[slot, HD:, :] = blank
        st[slot] = jnp.concatenate([scaled.astype(F32), blank_wide], 0).T.astype(BF)
    gq[...] = jnp.zeros_like(gq)
    gk[...] = jnp.zeros_like(gk)
    gv[...] = jnp.zeros_like(gv)

    def query_step(m, carry):
        i = plan[1 + m]

        def key_step(n, acc):
            j = plan[1 + n]
            score = dot(ks[j], qs[i])
            expo = jnp.exp2(score * SCALE2)
            through = dot(vs[j], ss[i])
            raw = (expo * (through - deltas[i])).astype(BF)
            gv[j] += dot(expo.astype(BF), st[i])
            gk[j] += dot(raw, qt[i])
            return acc + dot(kt[j], raw)

        gq[i] = lax.fori_loop(0, plan[0], key_step, jnp.zeros((HD, rows), F32))
        return carry

    lax.fori_loop(0, plan[0], query_step, 0)
    for slot, ref in enumerate((o0, o1, o2, o3)):
        ref[:HD, :] = (gq[slot] * SCALE).astype(BF)
        ref[HD : 2 * HD, :] = (gk[slot] * SCALE).T[:HD, :].astype(BF)
        ref[2 * HD :, :] = gv[slot].T[:HD, :].astype(BF)


def attend_back(plan, slabs, grads, kept, total, mask):
    rows = slabs[0].shape[1]
    return pl.pallas_call(
        attend_back_kernel,
        out_shape=tuple(sds((3 * HD, rows), BF) for _ in range(4)),
        in_specs=[SMEM] + [pl.BlockSpec()] * 11,
        scratch_shapes=[
            pltpu.VMEM((4, EXT, rows), BF),
            pltpu.VMEM((4, rows, EXT), BF),
            pltpu.VMEM((4, rows, EXT), BF),
            pltpu.VMEM((4, HD, rows), BF),
            pltpu.VMEM((4, rows, EXT), BF),
            pltpu.VMEM((4, EXT, rows), BF),
            pltpu.VMEM((4, rows, EXT), BF),
            pltpu.VMEM((4, 1, rows), F32),
            pltpu.VMEM((4, HD, rows), F32),
            pltpu.VMEM((4, rows, EXT), F32),
            pltpu.VMEM((4, rows, EXT), F32),
        ],
        name="attend_back",
    )(plan, *slabs, *grads, kept, total, mask)


def split_out(left, right, half, keep_a, keep_b, send_a, send_b):
    quarter = keep_a.shape[0]
    for value, lanes in ((left, slice(0, half)), (right, slice(half, 2 * half))):
        send_b[:, lanes] = value[3 * quarter :].astype(BF)
        send_a[:, lanes] = value[2 * quarter : 3 * quarter].astype(BF)
        keep_b[:, lanes] = value[quarter : 2 * quarter]
        keep_a[:, lanes] = value[:quarter]


def parts_shape(quarter, width):
    return (
        sds((quarter, width), F32),
        sds((quarter, width), F32),
        sds((quarter, width), BF),
        sds((quarter, width), BF),
    )


def output_kernel(ids, m0, m1, m2, m3, wa, wb, mixed_o, keep_a, keep_b, send_a, send_b, store):
    for slot, ref in enumerate((m0, m1, m2, m3)):
        begin = pl.multiple_of((ids[6] ^ slot) * HD, 16)
        store[pl.ds(begin, HD), :] = ref[...]
    mixed = store[...].astype(F32).T.astype(BF)
    mixed_o[...] = mixed
    half = wa.shape[0]
    split_out(
        dot_nt(mixed, wa[...]), dot_nt(mixed, wb[...]), half, keep_a, keep_b, send_a, send_b
    )


def output_part(ids, slabs, weights):
    rows = slabs[0].shape[1]
    half, width = weights[0].shape
    return pl.pallas_call(
        output_kernel,
        out_shape=(sds((rows, width), BF),) + parts_shape(rows // 4, 2 * half),
        in_specs=[SMEM] + [pl.BlockSpec()] * 6,
        scratch_shapes=[pltpu.VMEM((width, rows), BF)],
        name="output_part",
    )(ids, *slabs, *weights)


def middle_kernel(keep, first, second, frames, shift, gain, bias, middle_o, low_o):
    middle = (
        frames[...].astype(F32)
        + (keep[...] + first[...].astype(F32) + second[...].astype(F32))
        + shift[...]
    )
    middle_o[...] = middle
    unit, _ = normalize(middle)
    low_o[...] = (unit * gain[...] + bias[...]).astype(BF)


def middle_norm(keep, first, second, frames, shift, gain, bias):
    shape = keep.shape
    return pl.pallas_call(
        middle_kernel, out_shape=(sds(shape, F32), sds(shape, BF)), name="middle_norm"
    )(keep, first, second, frames, shift, gain, bias)


def feed_kernel(
    n0,
    n1,
    n2,
    n3,
    low,
    ia,
    ib,
    oa,
    ob,
    shift,
    normed_o,
    active_o,
    inner_o,
    shift_o,
    fa,
    fb,
    fc,
    fd,
    ba,
    bb,
    bc,
    bd,
    acc_f,
    acc_b,
):
    step = pl.program_id(0)
    half = ia.shape[0]
    quarter = n0.shape[0]

    @pl.when(step == 0)
    def _():
        for slot, ref in enumerate((n0, n1, n2, n3)):
            normed_o[slot * quarter : (slot + 1) * quarter, :] = ref[...]
        acc_f[...] = jnp.zeros_like(acc_f)
        acc_b[...] = jnp.zeros_like(acc_b)

    inner = dot(normed_o[:, :half], ia[...]) + dot(normed_o[:, half:], ib[...]) + shift[...]
    chance = 0.5 * (1.0 + lax.erf(inner * math.sqrt(0.5)))
    active = (inner * chance).astype(BF)
    active_o[...] = active
    slope = chance + inner * jnp.exp(-0.5 * inner * inner) * (1.0 / math.sqrt(2.0 * math.pi))
    grad = (dot(low[:, :half], oa[...]) + dot(low[:, half:], ob[...])) * slope
    shift_o[...] = jnp.sum(grad, 0, keepdims=True)
    grad_low = grad.astype(BF)
    inner_o[...] = grad_low
    acc_b[:, :half] += dot_nt(grad_low, ia[...])
    acc_b[:, half:] += dot_nt(grad_low, ib[...])
    acc_f[:, :half] += dot_nt(active, oa[...])
    acc_f[:, half:] += dot_nt(active, ob[...])

    @pl.when(step == pl.num_programs(0) - 1)
    def _():
        split_out(acc_b[:, :half], acc_b[:, half:], half, ba, bb, bc, bd)
        split_out(acc_f[:, :half], acc_f[:, half:], half, fa, fb, fc, fd)


def feed(parts, low, inner, outer, shift):
    quarter, width = parts[0].shape
    rows = 4 * quarter
    half, hidden = inner[0].shape
    block = 256
    whole = lambda *shape: pl.BlockSpec(shape, lambda f: (0,) * len(shape))
    cols = lambda count: pl.BlockSpec((count, block), lambda f: (0, f))
    part = whole(quarter, width)
    return pl.pallas_call(
        feed_kernel,
        grid=(hidden // block,),
        out_shape=(
            sds((rows, width), BF),
            sds((rows, hidden), BF),
            sds((rows, hidden), BF),
            sds((1, hidden), F32),
        )
        + parts_shape(quarter, width)
        + parts_shape(quarter, width),
        in_specs=[part] * 4 + [whole(rows, width)] + [cols(half)] * 4 + [cols(1)],
        out_specs=(whole(rows, width), cols(rows), cols(rows), cols(1)) + (part,) * 8,
        scratch_shapes=[pltpu.VMEM((rows, width), F32), pltpu.VMEM((rows, width), F32)],
        name="feed",
    )(*parts, low, *inner, *outer, shift)


def middle_back_kernel(
    keep, first, second, middle, final, gain, grad_o, low_o, gain_o, bias_o, shift_o
):
    grad = keep[...] + first[...].astype(F32) + second[...].astype(F32)
    unit, inverse = normalize(middle[...])
    gain_o[...] = jnp.sum(grad * unit, 0, keepdims=True)
    bias_o[...] = jnp.sum(grad, 0, keepdims=True)
    total = final[...].astype(F32) + norm_back(unit, inverse, grad, gain[...])
    grad_o[...] = total
    low_o[...] = total.astype(BF)
    shift_o[...] = jnp.sum(total, 0, keepdims=True)


def middle_back(keep, first, second, middle, final, gain):
    shape = keep.shape
    line = sds((1, shape[1]), F32)
    return pl.pallas_call(
        middle_back_kernel,
        out_shape=(sds(shape, F32), sds(shape, BF), line, line, line),
        name="middle_back",
    )(keep, first, second, middle, final, gain)


def attended_kernel(ids, l0, l1, l2, l3, wa, wb, low_o, o0, o1, o2, o3, store):
    half = wa.shape[0]
    quarter = l0.shape[0]
    for slot, ref in enumerate((l0, l1, l2, l3)):
        low_o[slot * quarter : (slot + 1) * quarter, :] = ref[...]
    value = dot(low_o[:, :half], wa[...]) + dot(low_o[:, half:], wb[...])
    store[...] = value.T.astype(BF)
    heads_out(ids, store, 0, (o0, o1, o2, o3), 4, HD)


def attended_grad(ids, parts, weights):
    quarter, width = parts[0].shape
    rows = 4 * quarter
    group = weights[0].shape[1]
    return pl.pallas_call(
        attended_kernel,
        out_shape=(sds((rows, width), BF),) + tuple(sds((HD, rows), BF) for _ in range(4)),
        in_specs=[SMEM] + [pl.BlockSpec()] * 6,
        scratch_shapes=[pltpu.VMEM((group, rows), BF)],
        name="attended_grad",
    )(ids, *parts, *weights)


def project_back_kernel(
    ids,
    s0,
    s1,
    s2,
    s3,
    qa,
    qb,
    ka,
    kb,
    va,
    vb,
    gq,
    gk,
    gv,
    q_sum,
    v_sum,
    keep_a,
    keep_b,
    send_a,
    send_b,
    store,
):
    half = qa.shape[0]
    left = None
    right = None
    for order, (first, second, out, total) in enumerate(
        ((qa, qb, gq, q_sum), (ka, kb, gk, None), (va, vb, gv, v_sum))
    ):
        for slot, ref in enumerate((s0, s1, s2, s3)):
            begin = pl.multiple_of((ids[6] ^ slot) * HD, 16)
            store[pl.ds(begin, HD), :] = ref[order * HD : (order + 1) * HD, :]
        wide = store[...].astype(F32).T
        grad = wide.astype(BF)
        out[...] = grad
        if total is not None:
            total[...] = jnp.sum(wide, 0, keepdims=True)
        term_left = dot_nt(grad, first[...])
        term_right = dot_nt(grad, second[...])
        left = term_left if left is None else left + term_left
        right = term_right if right is None else right + term_right
    split_out(left, right, half, keep_a, keep_b, send_a, send_b)


def project_back(ids, slabs, weights):
    rows = slabs[0].shape[1]
    half, group = weights[0].shape
    return pl.pallas_call(
        project_back_kernel,
        out_shape=tuple(sds((rows, group), BF) for _ in range(3))
        + (sds((1, group), F32), sds((1, group), F32))
        + parts_shape(rows // 4, 2 * half),
        in_specs=[SMEM] + [pl.BlockSpec()] * 10,
        scratch_shapes=[pltpu.VMEM((group, rows), BF)],
        name="project_back",
    )(ids, *slabs, *weights)


def first_back_kernel(keep, first, second, frames, middle_grad, gain, out_o, gain_o, bias_o):
    grad = keep[...] + first[...].astype(F32) + second[...].astype(F32)
    unit, inverse = normalize(frames[...].astype(F32))
    gain_o[...] = jnp.sum(grad * unit, 0, keepdims=True)
    bias_o[...] = jnp.sum(grad, 0, keepdims=True)
    out_o[...] = (middle_grad[...] + norm_back(unit, inverse, grad, gain[...])).astype(BF)


def first_back(keep, first, second, frames, middle_grad, gain):
    shape = keep.shape
    line = sds((1, shape[1]), F32)
    return pl.pallas_call(
        first_back_kernel, out_shape=(sds(shape, BF), line, line), name="first_back"
    )(keep, first, second, frames, middle_grad, gain)


def gather_kernel(ids, *refs):
    out = refs[-1]
    micro = pl.program_id(0)
    piece = pl.program_id(1)
    half = out.shape[-1] // 2
    for m in range(len(refs) // 4):
        for p in range(4):

            @pl.when((micro == m) & (piece == p))
            def _(ref=refs[4 * m + p]):
                left = ref[:, :half]
                right = ref[:, half:]

                @pl.when(ids[4] == 0)
                def _():
                    out[0, 0, :, :half] = left
                    out[0, 0, :, half:] = right

                @pl.when(ids[4] != 0)
                def _():
                    out[0, 0, :, :half] = right
                    out[0, 0, :, half:] = left


def gather_rows(ids, parts):
    quarter, width = parts[0].shape
    micros = len(parts) // 4
    return pl.pallas_call(
        gather_kernel,
        out_shape=sds((micros, 1, 4 * quarter, width), BF),
        grid_spec=pltpu.PrefetchScalarGridSpec(
            num_scalar_prefetch=1,
            grid=(micros, 4),
            in_specs=[pl.BlockSpec((quarter, width), lambda m, p, ids: (0, 0))] * len(parts),
            out_specs=pl.BlockSpec((1, 1, quarter, width), lambda m, p, ids: (m, 0, ids[p], 0)),
        ),
        name="gather_rows",
    )(ids, *parts)


def per_device(
    sizes,
    frames,
    lengths,
    first_gain,
    first_bias,
    query_weight,
    query_bias,
    key_weight,
    value_weight,
    value_bias,
    output_weight,
    output_bias,
    second_gain,
    second_bias,
    inner_weight,
    inner_bias,
    outer_weight,
    outer_bias,
    cotangent,
):
    shard_count = sizes["shard"]
    ctx_count = sizes["ctx"]
    tp_count = sizes["tp"]
    assert ctx_count == 4 and tp_count == 4
    micros = frames.shape[0]
    rows = frames.shape[2]
    width = frames.shape[3]
    half = width // 2
    quarter = rows // 4
    paired = shard_count == 2
    tp_at = lax.axis_index("tp")
    ctx_at = lax.axis_index("ctx")
    shard_at = lax.axis_index("shard") if paired else jnp.int32(0)

    def core(value):
        return lax.ppermute(value, "tp", [(i, i ^ 1) for i in range(4)])

    def across(value):
        return lax.ppermute(value, "tp", [(i, i ^ 2) for i in range(4)])

    def blocks(value, slot):
        return lax.ppermute(value, "ctx", [(i, i ^ slot) for i in range(4)])

    def mate(value):
        return lax.ppermute(value, "shard", [(0, 1), (1, 0)])

    order = [tp_at ^ slot for slot in SLOTS]
    ids = jnp.stack(
        [jnp.int32(v) for v in order]
        + [shard_at, 1 - shard_at if paired else jnp.int32(1), ctx_at, tp_at]
        + [lengths[m, 0] for m in range(micros)]
    ).astype(jnp.int32)

    def turn(line):
        if not paired:
            return line
        return jnp.where(shard_at == 0, line, jnp.roll(line, half, -1))

    def line_of(vector):
        return turn(vector.astype(F32)[None, :])

    gain_one = line_of(first_gain)
    bias_one = line_of(first_bias)
    gain_two = line_of(second_gain)
    bias_two = line_of(second_bias)
    output_shift = line_of(output_bias)
    outer_shift = line_of(outer_bias)
    query_shift = query_bias.astype(F32)[None, :]
    value_shift = value_bias.astype(F32)[None, :]
    inner_shift = inner_bias.astype(F32)[None, :]

    held = {}

    def fetch(name, weight, after=None):
        if paired:
            if after is not None:
                weight, _ = lax.optimization_barrier((weight, after))
            held[name] = (weight, mate(weight))
        else:
            full = lax.all_gather(weight, "shard", axis=0, tiled=True)
            held[name] = (full[:half], full[half:])
        return held[name][1]

    got_q = fetch("query", query_weight)
    got_k = fetch("key", key_weight)
    got_v = fetch("value", value_weight)
    got_o = fetch("output", output_weight, got_k)
    got_w = fetch("outer", outer_weight, got_v)
    fetch("inner", inner_weight, got_o)
    qkv = held["query"] + held["key"] + held["value"]

    frames_in = frames[:, 0]
    cotangent_in = cotangent[:, 0]
    offsets = jnp.concatenate(
        [quarter * v + jnp.arange(quarter, dtype=jnp.int32) for v in order]
    )

    def cut_own(array, m):
        return turn(lax.dynamic_slice_in_dim(array[m], order[0] * quarter, quarter, 0))

    def reduce_rows(parts):
        keep_a, keep_b, send_a, send_b = parts
        near_b = core(send_b)
        near_a = core(send_a)
        far = across((keep_b + near_b.astype(F32)).astype(BF))
        return keep_a, near_a, far

    def spread_rows(own):
        far = across(own)
        near = core(own)
        return own, far, near, core(far)

    def exchange(slabs):
        return (slabs[0],) + tuple(blocks(slabs[s], s) for s in range(1, 4))

    state = [dict() for _ in range(micros)]
    for m in range(micros):
        s = state[m]
        length = lengths[m, 0]
        s["normed"], s["low"] = front(m, ids, frames_in, cotangent_in, gain_one, bias_one)
        s["own"] = cut_own(frames_in, m)
        starts = jnp.stack([(ctx_at ^ slot) * rows for slot in range(4)])
        s["mask"] = jnp.where(
            starts[:, None, None] + offsets[None, None, :] < length, 0.0, -1e30
        ).astype(F32)
        live = (starts < length).astype(jnp.int32)
        places = jnp.cumsum(live) - live
        listed = jnp.sum(
            jnp.where(
                (live[None, :] == 1) & (places[None, :] == jnp.arange(4)[:, None]),
                jnp.arange(4)[None, :],
                0,
            ),
            -1,
        )
        s["plan"] = jnp.concatenate([jnp.sum(live)[None], listed]).astype(jnp.int32)
    for m in range(micros):
        s = state[m]
        s["slabs"] = exchange(project(ids, s["normed"], qkv, query_shift, value_shift))
    for m in range(micros):
        s = state[m]
        found = attend(s["plan"], s["slabs"], s["mask"])
        s["kept"], s["total"] = found[4:]
        s["heads"] = exchange(found[:4])
    for m in range(micros):
        s = state[m]
        s["mixed"], *parts = output_part(ids, s["heads"], held["output"])
        s["middle"], low_two = middle_norm(
            *reduce_rows(parts), s["own"], output_shift, gain_two, bias_two
        )
        s["spread"] = spread_rows(low_two)
    for m in range(micros):
        s = state[m]
        found = feed(s["spread"], s["low"], held["inner"], held["outer"], inner_shift)
        s["normed_two"], s["active"], s["inner"], s["inner_sum"] = found[:4]
        s["forward"] = found[4:8]
        s["final_own"] = s["low"][:quarter]
        keep, near, far = reduce_rows(found[8:])
        s["grad_middle"], low_middle, s["gain_two"], s["bias_two"], s["shift_out"] = middle_back(
            keep, near, far, s["middle"], s["final_own"], gain_two
        )
        s["low_parts"] = spread_rows(low_middle)
    for m in range(micros):
        s = state[m]
        s["low_middle"], *slabs = attended_grad(ids, s["low_parts"], held["output"])
        s["head_grads"] = exchange(slabs)

    def weight_grad(lefts, rights):
        if paired:
            away = sum(dot_tn(a[:, half:], b) for a, b in zip(lefts, rights))
            came = mate(away.astype(BF))
            home = sum(dot_tn(a[:, :half], b) for a, b in zip(lefts, rights))
            total = home + came.astype(F32)
        else:
            full = sum(dot_tn(a, b) for a, b in zip(lefts, rights))
            total = lax.psum_scatter(
                full.astype(BF), "shard", scatter_dimension=0, tiled=True
            ).astype(F32)
        return total.astype(BF)

    inner_pair = (ctx_at == 1) | (ctx_at == 2)

    def over_blocks(value):
        first = lax.ppermute(value, "ctx", [(0, 1), (3, 2)])
        part = (value.astype(F32) + first.astype(F32)).astype(BF)
        second = lax.ppermute(part, "ctx", [(1, 2), (2, 1)])
        whole = (part.astype(F32) + second.astype(F32)).astype(BF)
        third = lax.ppermute(whole, "ctx", [(1, 0), (2, 3)])
        return jnp.where(inner_pair, whole, third).astype(F32)

    def in_pieces(value, count):
        step = value.shape[0] // count
        return jnp.concatenate(
            [over_blocks(value[i * step : (i + 1) * step]) for i in range(count)], 0
        )

    grads = {}
    pieces = 2 if (width // shard_count) % 32 == 0 else 1
    every = lambda name: [s[name] for s in state]
    grads["outer"] = in_pieces(weight_grad(every("low"), every("active")), pieces)
    grads["inner"] = in_pieces(weight_grad(every("normed_two"), every("inner")), pieces)
    grads["output"] = over_blocks(weight_grad(every("low_middle"), every("mixed")))
    for m in range(micros):
        s = state[m]
        s["back"] = exchange(
            attend_back(s["plan"], s["slabs"], s["head_grads"], s["kept"], s["total"], s["mask"])
        )
    for m in range(micros):
        s = state[m]
        found = project_back(ids, s["back"], qkv)
        s["gq"], s["gk"], s["gv"], s["q_sum"], s["v_sum"] = found[:5]
        keep, near, far = reduce_rows(found[5:])
        out, s["gain_one"], s["bias_one"] = first_back(
            keep, near, far, s["own"], s["grad_middle"], gain_one
        )
        s["frames_grad"] = spread_rows(out)
    grads["key"] = over_blocks(weight_grad(every("normed"), every("gk")))
    grads["value"] = over_blocks(weight_grad(every("normed"), every("gv")))
    grads["query"] = over_blocks(weight_grad(every("normed"), every("gq")))
    for m in range(micros):
        s = state[m]
        keep, near, far = reduce_rows(s["forward"])
        final = (
            s["middle"] + (keep + near.astype(F32) + far.astype(F32)) + outer_shift
        ).astype(BF)
        s["result"] = spread_rows(final)
    result = gather_rows(ids, sum((s["result"] for s in state), ()))
    frames_grad = gather_rows(ids, sum((s["frames_grad"] for s in state), ()))

    def over_all(value):
        value = value + core(value)
        return value + across(value)

    def over_frames(value):
        value = value + mate(value) if paired else lax.psum(value, "shard")
        value = value + blocks(value, 1)
        return value + blocks(value, 2)

    def both(name):
        return sum(every(name))

    shift_final = sum(
        jnp.sum(s["final_own"].astype(F32), 0, keepdims=True) for s in state
    )
    small = jnp.concatenate(
        [
            turn(both("gain_one")),
            turn(both("bias_one")),
            turn(both("gain_two")),
            turn(both("bias_two")),
            turn(both("shift_out")),
            turn(shift_final),
        ],
        0,
    )
    small = over_all(small)
    group = query_weight.shape[1]
    hidden = inner_weight.shape[1]
    narrow = jnp.concatenate([both("inner_sum"), both("q_sum"), both("v_sum")], 1)
    room = -narrow.shape[1] % width
    narrow = jnp.pad(narrow, ((0, 0), (0, room))).reshape(-1, width)
    small = over_frames(jnp.concatenate([small, narrow], 0))
    narrow = small[6:].reshape(-1)
    return (
        result,
        frames_grad,
        small[0],
        small[1],
        grads["query"],
        narrow[hidden : hidden + group],
        grads["key"],
        grads["value"],
        narrow[hidden + group : hidden + 2 * group],
        grads["output"],
        small[4],
        small[2],
        small[3],
        grads["inner"],
        narrow[:hidden],
        grads["outer"],
        small[5],
    )


def solution(mesh):
    split = P(None, "shard", "ctx", None)
    cut = P("shard", "tp")
    ins = (split, P(None, "shard"), P(), P(), cut, P("tp"), cut, cut, P("tp"), cut)
    ins += (P(), P(), P(), cut, P("tp"), cut, P(), split)
    outs = (split, split, P(), P(), cut, P("tp"), cut, cut, P("tp"), cut)
    outs += (P(), P(), P(), cut, P("tp"), cut, P())
    return jax.shard_map(
        functools.partial(per_device, dict(mesh.shape)),
        mesh=mesh,
        in_specs=ins,
        out_specs=outs,
        check_vma=False,
    )
```

```python
import functools
import math
import types

import jax
import jax.numpy as jnp
from jax import lax
from jax.experimental import pallas as pl
from jax.experimental.pallas import tpu as pltpu
from jax.sharding import PartitionSpec as P


HD = 80
EXT = 96
EPS = 1e-05
BF = jnp.bfloat16
F32 = jnp.float32
SCALE = 1.0 / math.sqrt(HD)
SCALE2 = SCALE * math.log2(math.e)
SLOTS = (0, 2, 1, 3)
NT = (((1,), (1,)), ((), ()))
TN = (((0,), (0,)), ((), ()))


def sds(shape, kind):
    return jax.ShapeDtypeStruct(shape, kind)


def dot(left, right):
    return jnp.dot(left, right, preferred_element_type=F32)


def dot_nt(left, right):
    return lax.dot_general(left, right, NT, preferred_element_type=F32)


def dot_tn(left, right):
    return lax.dot_general(left, right, TN, preferred_element_type=F32)


def tie(value, *others):
    return lax.optimization_barrier((value,) + others)[0]


def normalize(values):
    center = values - jnp.mean(values, -1, keepdims=True)
    spread = jnp.mean(center * center, -1, keepdims=True)
    inverse = lax.rsqrt(spread + EPS)
    return center * inverse, inverse


def norm_back(unit, inverse, grad, gain):
    scaled = grad * gain
    first = jnp.mean(scaled, -1, keepdims=True)
    second = jnp.mean(scaled * unit, -1, keepdims=True)
    return inverse * (scaled - first - unit * second)


SMEM = pl.BlockSpec(memory_space=pltpu.SMEM)


def front_kernel(micro, ids, fa, fb, ca, cb, gain, bias, normed_o, low_o):
    half = fa.shape[-1]
    rows = fa.shape[-2]
    piece = pl.program_id(0)
    va = fa[0].astype(F32)
    vb = fb[0].astype(F32)
    count = 2 * half
    mean = (jnp.sum(va, -1, keepdims=True) + jnp.sum(vb, -1, keepdims=True)) / count
    va = va - mean
    vb = vb - mean
    spread = (jnp.sum(va * va, -1, keepdims=True) + jnp.sum(vb * vb, -1, keepdims=True)) / count
    inverse = lax.rsqrt(spread + EPS)
    normed_o[:, :half] = (va * inverse * gain[:, :half] + bias[:, :half]).astype(BF)
    normed_o[:, half:] = (vb * inverse * gain[:, half:] + bias[:, half:]).astype(BF)
    start = ids[6] * (rows * 4) + ids[piece] * rows
    valid = start + lax.broadcasted_iota(jnp.int32, (rows, 1), 0) < ids[8 + micro]
    low_o[:, :half] = jnp.where(valid, ca[0].astype(F32), 0.0).astype(BF)
    low_o[:, half:] = jnp.where(valid, cb[0].astype(F32), 0.0).astype(BF)


def front(micro, ids, frames, cotangent, gain, bias):
    rows, width = frames.shape[1:]
    quarter = rows // 4
    half = width // 2
    own = pl.BlockSpec((1, quarter, half), lambda p, ids: (micro, ids[p], ids[4]))
    other = pl.BlockSpec((1, quarter, half), lambda p, ids: (micro, ids[p], ids[5]))
    line = pl.BlockSpec((1, width), lambda p, ids: (0, 0))
    out = pl.BlockSpec((quarter, width), lambda p, ids: (p, 0))
    return pl.pallas_call(
        functools.partial(front_kernel, micro),
        out_shape=(sds((rows, width), BF), sds((rows, width), BF)),
        grid_spec=pltpu.PrefetchScalarGridSpec(
            num_scalar_prefetch=1,
            grid=(4,),
            in_specs=[own, other, own, other, line, line],
            out_specs=[out, out],
        ),
    )(ids, frames, frames, cotangent, cotangent, gain, bias)


def heads_out(ids, store, offset, outs):
    for slot in range(len(outs)):
        begin = pl.multiple_of((ids[6] ^ slot) * HD, 16)
        outs[slot][offset : offset + HD, :] = store[pl.ds(begin, HD), :]


def project_kernel(ids, normed, qa, qb, ka, kb, va, vb, q_bias, v_bias, o0, o1, o2, o3, store):
    half = qa.shape[0]
    left = normed[:, :half]
    right = normed[:, half:]
    outs = (o0, o1, o2, o3)
    for order, (first, second, shift) in enumerate(
        ((qa, qb, q_bias), (ka, kb, None), (va, vb, v_bias))
    ):
        value = dot(left, first[...]) + dot(right, second[...])
        if shift is not None:
            value = value + shift[...]
        store[...] = value.T.astype(BF)
        heads_out(ids, store, order * HD, outs)


def project(ids, normed, weights, q_bias, v_bias):
    rows = normed.shape[0]
    width = weights[0].shape[1]
    return pl.pallas_call(
        project_kernel,
        out_shape=tuple(sds((3 * HD, rows), BF) for _ in range(4)),
        in_specs=[SMEM] + [pl.BlockSpec()] * 9,
        scratch_shapes=[pltpu.VMEM((width, rows), BF)],
    )(ids, normed, *weights, q_bias, v_bias)


def attend_kernel(plan, x0, x1, x2, x3, mask, o0, o1, o2, o3, kept, total, qs, ks, vs):
    rows = x0.shape[1]
    tail = EXT - HD
    first = lax.broadcasted_iota(jnp.int32, (tail, rows), 0) == 0
    ones = jnp.where(first, 1.0, 0.0).astype(BF)
    for slot, ref in enumerate((x0, x1, x2, x3)):
        qs[slot, :HD, :] = ref[:HD, :]
        qs[slot, HD:, :] = ones
        vs[slot, :HD, :] = ref[2 * HD :, :]
        vs[slot, HD:, :] = ones
        shift = jnp.where(first, mask[slot], 0.0)
        whole = jnp.concatenate([ref[HD : 2 * HD, :].astype(F32), shift], 0)
        ks[slot] = whole.T.astype(BF)
    has = plan[0] > 0

    def query_step(i, carry):
        query = qs[i]

        def key_step(n, acc):
            j = plan[1 + n]
            score = dot(ks[j], query)
            expo = jnp.exp2(score * SCALE2).astype(BF)
            return acc + dot(vs[j], expo)

        acc = lax.fori_loop(0, plan[0], key_step, jnp.zeros((EXT, rows), F32))
        denom = jnp.where(has, acc[HD : HD + 1, :], 1.0)
        attended = acc[:HD, :] / denom
        kept[i] = attended
        total[i] = denom
        return carry

    lax.fori_loop(0, 4, query_step, 0)
    for slot, ref in enumerate((o0, o1, o2, o3)):
        ref[...] = kept[slot].astype(BF)


def attend(plan, slabs, mask):
    rows = slabs[0].shape[1]
    return pl.pallas_call(
        attend_kernel,
        out_shape=tuple(sds((HD, rows), BF) for _ in range(4))
        + (sds((4, HD, rows), F32), sds((4, 1, rows), F32)),
        in_specs=[SMEM] + [pl.BlockSpec()] * 5,
        scratch_shapes=[
            pltpu.VMEM((4, EXT, rows), BF),
            pltpu.VMEM((4, rows, EXT), BF),
            pltpu.VMEM((4, EXT, rows), BF),
        ],
    )(plan, *slabs, mask)


def attend_back_kernel(
    plan,
    x0,
    x1,
    x2,
    x3,
    g0,
    g1,
    g2,
    g3,
    kept,
    total,
    mask,
    o0,
    o1,
    o2,
    o3,
    qs,
    qt,
    ks,
    kt,
    vs,
    ss,
    st,
    deltas,
    gq,
    gk,
    gv,
):
    rows = x0.shape[1]
    tail = EXT - HD
    first = lax.broadcasted_iota(jnp.int32, (tail, rows), 0) == 0
    ones = jnp.where(first, 1.0, 0.0).astype(BF)
    blank = jnp.zeros((tail, rows), BF)
    blank_wide = jnp.zeros((tail, rows), F32)
    for slot, (ref, grad_ref) in enumerate(zip((x0, x1, x2, x3), (g0, g1, g2, g3))):
        qs[slot, :HD, :] = ref[:HD, :]
        qs[slot, HD:, :] = ones
        qt[slot] = jnp.concatenate([ref[:HD, :].astype(F32), blank_wide], 0).T.astype(BF)
        kt[slot] = ref[HD : 2 * HD, :]
        shift = jnp.where(first, mask[slot], 0.0)
        ks[slot] = jnp.concatenate([ref[HD : 2 * HD, :].astype(F32), shift], 0).T.astype(BF)
        vs[slot] = jnp.concatenate([ref[2 * HD :, :].astype(F32), blank_wide], 0).T.astype(BF)
        grad = grad_ref[...].astype(F32)
        recip = 1.0 / total[slot]
        deltas[slot] = jnp.sum(grad * kept[slot], 0, keepdims=True) * recip
        scaled = (grad * recip).astype(BF)
        ss[slot, :HD, :] = scaled
        ss[slot, HD:, :] = blank
        st[slot] = jnp.concatenate([scaled.astype(F32), blank_wide], 0).T.astype(BF)
    gq[...] = jnp.zeros_like(gq)
    gk[...] = jnp.zeros_like(gk)
    gv[...] = jnp.zeros_like(gv)

    def query_step(m, carry):
        i = plan[1 + m]

        def key_step(n, acc):
            j = plan[1 + n]
            score = dot(ks[j], qs[i])
            expo = jnp.exp2(score * SCALE2)
            through = dot(vs[j], ss[i])
            raw = (expo * (through - deltas[i])).astype(BF)
            gv[j] += dot(expo.astype(BF), st[i])
            gk[j] += dot(raw, qt[i])
            return acc + dot(kt[j], raw)

        gq[i] = lax.fori_loop(0, plan[0], key_step, jnp.zeros((HD, rows), F32))
        return carry

    lax.fori_loop(0, plan[0], query_step, 0)
    for slot, ref in enumerate((o0, o1, o2, o3)):
        ref[:HD, :] = (gq[slot] * SCALE).astype(BF)
        ref[HD : 2 * HD, :] = (gk[slot] * SCALE).T[:HD, :].astype(BF)
        ref[2 * HD :, :] = gv[slot].T[:HD, :].astype(BF)


def attend_back(plan, slabs, grads, kept, total, mask):
    rows = slabs[0].shape[1]
    return pl.pallas_call(
        attend_back_kernel,
        out_shape=tuple(sds((3 * HD, rows), BF) for _ in range(4)),
        in_specs=[SMEM] + [pl.BlockSpec()] * 11,
        scratch_shapes=[
            pltpu.VMEM((4, EXT, rows), BF),
            pltpu.VMEM((4, rows, EXT), BF),
            pltpu.VMEM((4, rows, EXT), BF),
            pltpu.VMEM((4, HD, rows), BF),
            pltpu.VMEM((4, rows, EXT), BF),
            pltpu.VMEM((4, EXT, rows), BF),
            pltpu.VMEM((4, rows, EXT), BF),
            pltpu.VMEM((4, 1, rows), F32),
            pltpu.VMEM((4, HD, rows), F32),
            pltpu.VMEM((4, rows, EXT), F32),
            pltpu.VMEM((4, rows, EXT), F32),
        ],
    )(plan, *slabs, *grads, kept, total, mask)


def split_out(left, right, half, keep_a, keep_b, send_a, send_b):
    quarter = keep_a.shape[0]
    for value, lanes in ((left, slice(0, half)), (right, slice(half, 2 * half))):
        send_b[:, lanes] = value[3 * quarter :].astype(BF)
        send_a[:, lanes] = value[2 * quarter : 3 * quarter].astype(BF)
        keep_b[:, lanes] = value[quarter : 2 * quarter]
        keep_a[:, lanes] = value[:quarter]


def parts_shape(quarter, width):
    return (
        sds((quarter, width), F32),
        sds((quarter, width), F32),
        sds((quarter, width), BF),
        sds((quarter, width), BF),
    )


def output_kernel(ids, m0, m1, m2, m3, wa, wb, mixed_o, keep_a, keep_b, send_a, send_b, store):
    for slot, ref in enumerate((m0, m1, m2, m3)):
        begin = pl.multiple_of((ids[6] ^ slot) * HD, 16)
        store[pl.ds(begin, HD), :] = ref[...]
    mixed = store[...].astype(F32).T.astype(BF)
    mixed_o[...] = mixed
    half = wa.shape[0]
    split_out(
        dot_nt(mixed, wa[...]), dot_nt(mixed, wb[...]), half, keep_a, keep_b, send_a, send_b
    )


def output_part(ids, slabs, weights):
    rows = slabs[0].shape[1]
    half, width = weights[0].shape
    return pl.pallas_call(
        output_kernel,
        out_shape=(sds((rows, width), BF),) + parts_shape(rows // 4, 2 * half),
        in_specs=[SMEM] + [pl.BlockSpec()] * 6,
        scratch_shapes=[pltpu.VMEM((width, rows), BF)],
    )(ids, *slabs, *weights)


def middle_kernel(keep, first, second, frames, shift, gain, bias, middle_o, low_o):
    middle = (
        frames[...].astype(F32)
        + (keep[...] + first[...].astype(F32) + second[...].astype(F32))
        + shift[...]
    )
    middle_o[...] = middle
    unit, _ = normalize(middle)
    low_o[...] = (unit * gain[...] + bias[...]).astype(BF)


def middle_norm(keep, first, second, frames, shift, gain, bias):
    shape = keep.shape
    return pl.pallas_call(
        middle_kernel, out_shape=(sds(shape, F32), sds(shape, BF))
    )(keep, first, second, frames, shift, gain, bias)


def feed_kernel(
    n0,
    n1,
    n2,
    n3,
    low,
    ia,
    ib,
    oa,
    ob,
    shift,
    normed_o,
    active_o,
    inner_o,
    shift_o,
    fa,
    fb,
    fc,
    fd,
    ba,
    bb,
    bc,
    bd,
    acc_f,
    acc_b,
):
    step = pl.program_id(0)
    half = ia.shape[0]
    quarter = n0.shape[0]

    @pl.when(step == 0)
    def _():
        for slot, ref in enumerate((n0, n1, n2, n3)):
            normed_o[slot * quarter : (slot + 1) * quarter, :] = ref[...]
        acc_f[...] = jnp.zeros_like(acc_f)
        acc_b[...] = jnp.zeros_like(acc_b)

    inner = dot(normed_o[:, :half], ia[...]) + dot(normed_o[:, half:], ib[...]) + shift[...]
    chance = 0.5 * (1.0 + lax.erf(inner * math.sqrt(0.5)))
    active = (inner * chance).astype(BF)
    active_o[...] = active
    slope = chance + inner * jnp.exp(-0.5 * inner * inner) * (1.0 / math.sqrt(2.0 * math.pi))
    grad = (dot(low[:, :half], oa[...]) + dot(low[:, half:], ob[...])) * slope
    shift_o[...] = jnp.sum(grad, 0, keepdims=True)
    grad_low = grad.astype(BF)
    inner_o[...] = grad_low
    acc_b[:, :half] += dot_nt(grad_low, ia[...])
    acc_b[:, half:] += dot_nt(grad_low, ib[...])
    acc_f[:, :half] += dot_nt(active, oa[...])
    acc_f[:, half:] += dot_nt(active, ob[...])

    @pl.when(step == pl.num_programs(0) - 1)
    def _():
        split_out(acc_b[:, :half], acc_b[:, half:], half, ba, bb, bc, bd)
        split_out(acc_f[:, :half], acc_f[:, half:], half, fa, fb, fc, fd)


def feed(parts, low, inner, outer, shift):
    quarter, width = parts[0].shape
    rows = 4 * quarter
    half, hidden = inner[0].shape
    block = 256
    whole = lambda *shape: pl.BlockSpec(shape, lambda f: (0,) * len(shape))
    cols = lambda count: pl.BlockSpec((count, block), lambda f: (0, f))
    part = whole(quarter, width)
    return pl.pallas_call(
        feed_kernel,
        grid=(hidden // block,),
        out_shape=(
            sds((rows, width), BF),
            sds((rows, hidden), BF),
            sds((rows, hidden), BF),
            sds((1, hidden), F32),
        )
        + parts_shape(quarter, width)
        + parts_shape(quarter, width),
        in_specs=[part] * 4 + [whole(rows, width)] + [cols(half)] * 4 + [cols(1)],
        out_specs=(whole(rows, width), cols(rows), cols(rows), cols(1)) + (part,) * 8,
        scratch_shapes=[pltpu.VMEM((rows, width), F32), pltpu.VMEM((rows, width), F32)],
    )(*parts, low, *inner, *outer, shift)


def middle_back_kernel(
    keep, first, second, middle, final, gain, grad_o, low_o, gain_o, bias_o, shift_o
):
    grad = keep[...] + first[...].astype(F32) + second[...].astype(F32)
    unit, inverse = normalize(middle[...])
    gain_o[...] = jnp.sum(grad * unit, 0, keepdims=True)
    bias_o[...] = jnp.sum(grad, 0, keepdims=True)
    total = final[...].astype(F32) + norm_back(unit, inverse, grad, gain[...])
    grad_o[...] = total
    low_o[...] = total.astype(BF)
    shift_o[...] = jnp.sum(total, 0, keepdims=True)


def middle_back(keep, first, second, middle, final, gain):
    shape = keep.shape
    line = sds((1, shape[1]), F32)
    return pl.pallas_call(
        middle_back_kernel,
        out_shape=(sds(shape, F32), sds(shape, BF), line, line, line),
    )(keep, first, second, middle, final, gain)


def attended_kernel(ids, l0, l1, l2, l3, wa, wb, low_o, o0, o1, o2, o3, store):
    half = wa.shape[0]
    quarter = l0.shape[0]
    for slot, ref in enumerate((l0, l1, l2, l3)):
        low_o[slot * quarter : (slot + 1) * quarter, :] = ref[...]
    value = dot(low_o[:, :half], wa[...]) + dot(low_o[:, half:], wb[...])
    store[...] = value.T.astype(BF)
    heads_out(ids, store, 0, (o0, o1, o2, o3))


def attended_grad(ids, parts, weights):
    quarter, width = parts[0].shape
    rows = 4 * quarter
    group = weights[0].shape[1]
    return pl.pallas_call(
        attended_kernel,
        out_shape=(sds((rows, width), BF),) + tuple(sds((HD, rows), BF) for _ in range(4)),
        in_specs=[SMEM] + [pl.BlockSpec()] * 6,
        scratch_shapes=[pltpu.VMEM((group, rows), BF)],
    )(ids, *parts, *weights)


def project_back_kernel(
    ids,
    s0,
    s1,
    s2,
    s3,
    qa,
    qb,
    ka,
    kb,
    va,
    vb,
    gq,
    gk,
    gv,
    q_sum,
    v_sum,
    keep_a,
    keep_b,
    send_a,
    send_b,
    store,
):
    half = qa.shape[0]
    left = None
    right = None
    for order, (first, second, out, total) in enumerate(
        ((qa, qb, gq, q_sum), (ka, kb, gk, None), (va, vb, gv, v_sum))
    ):
        for slot, ref in enumerate((s0, s1, s2, s3)):
            begin = pl.multiple_of((ids[6] ^ slot) * HD, 16)
            store[pl.ds(begin, HD), :] = ref[order * HD : (order + 1) * HD, :]
        wide = store[...].astype(F32).T
        grad = wide.astype(BF)
        out[...] = grad
        if total is not None:
            total[...] = jnp.sum(wide, 0, keepdims=True)
        term_left = dot_nt(grad, first[...])
        term_right = dot_nt(grad, second[...])
        left = term_left if left is None else left + term_left
        right = term_right if right is None else right + term_right
    split_out(left, right, half, keep_a, keep_b, send_a, send_b)


def project_back(ids, slabs, weights):
    rows = slabs[0].shape[1]
    half, group = weights[0].shape
    return pl.pallas_call(
        project_back_kernel,
        out_shape=tuple(sds((rows, group), BF) for _ in range(3))
        + (sds((1, group), F32), sds((1, group), F32))
        + parts_shape(rows // 4, 2 * half),
        in_specs=[SMEM] + [pl.BlockSpec()] * 10,
        scratch_shapes=[pltpu.VMEM((group, rows), BF)],
    )(ids, *slabs, *weights)


def first_back_kernel(keep, first, second, frames, middle_grad, gain, out_o, gain_o, bias_o):
    grad = keep[...] + first[...].astype(F32) + second[...].astype(F32)
    unit, inverse = normalize(frames[...].astype(F32))
    gain_o[...] = jnp.sum(grad * unit, 0, keepdims=True)
    bias_o[...] = jnp.sum(grad, 0, keepdims=True)
    out_o[...] = (middle_grad[...] + norm_back(unit, inverse, grad, gain[...])).astype(BF)


def first_back(keep, first, second, frames, middle_grad, gain):
    shape = keep.shape
    line = sds((1, shape[1]), F32)
    return pl.pallas_call(
        first_back_kernel, out_shape=(sds(shape, BF), line, line)
    )(keep, first, second, frames, middle_grad, gain)


def gather_kernel(ids, *refs):
    out = refs[-1]
    micro = pl.program_id(0)
    piece = pl.program_id(1)
    half = out.shape[-1] // 2
    for m in range(len(refs) // 4):
        for p in range(4):

            @pl.when((micro == m) & (piece == p))
            def _(ref=refs[4 * m + p]):
                left = ref[:, :half]
                right = ref[:, half:]

                @pl.when(ids[4] == 0)
                def _():
                    out[0, 0, :, :half] = left
                    out[0, 0, :, half:] = right

                @pl.when(ids[4] != 0)
                def _():
                    out[0, 0, :, :half] = right
                    out[0, 0, :, half:] = left


def gather_rows(ids, parts):
    quarter, width = parts[0].shape
    micros = len(parts) // 4
    return pl.pallas_call(
        gather_kernel,
        out_shape=sds((micros, 1, 4 * quarter, width), BF),
        grid_spec=pltpu.PrefetchScalarGridSpec(
            num_scalar_prefetch=1,
            grid=(micros, 4),
            in_specs=[pl.BlockSpec((quarter, width), lambda m, p, ids: (0, 0))] * len(parts),
            out_specs=pl.BlockSpec((1, 1, quarter, width), lambda m, p, ids: (m, 0, ids[p], 0)),
        ),
    )(ids, *parts)


def per_device(
    sizes,
    frames,
    lengths,
    first_gain,
    first_bias,
    query_weight,
    query_bias,
    key_weight,
    value_weight,
    value_bias,
    output_weight,
    output_bias,
    second_gain,
    second_bias,
    inner_weight,
    inner_bias,
    outer_weight,
    outer_bias,
    cotangent,
):
    shard_count = sizes["shard"]
    ctx_count = sizes["ctx"]
    tp_count = sizes["tp"]
    assert ctx_count == 4 and tp_count == 4
    micros = frames.shape[0]
    rows = frames.shape[2]
    width = frames.shape[3]
    half = width // 2
    quarter = rows // 4
    paired = shard_count == 2
    tp_at = lax.axis_index("tp")
    ctx_at = lax.axis_index("ctx")
    shard_at = lax.axis_index("shard") if paired else jnp.int32(0)

    def core(value):
        return lax.ppermute(value, "tp", [(i, i ^ 1) for i in range(4)])

    def across(value):
        return lax.ppermute(value, "tp", [(i, i ^ 2) for i in range(4)])

    def blocks(value, slot):
        return lax.ppermute(value, "ctx", [(i, i ^ slot) for i in range(4)])

    def mate(value):
        return lax.ppermute(value, "shard", [(0, 1), (1, 0)])

    order = [tp_at ^ slot for slot in SLOTS]
    ids = jnp.stack(
        [jnp.int32(v) for v in order]
        + [shard_at, 1 - shard_at if paired else jnp.int32(1), ctx_at, tp_at]
        + [lengths[m, 0] for m in range(micros)]
    ).astype(jnp.int32)

    def turn(line):
        if not paired:
            return line
        return jnp.where(shard_at == 0, line, jnp.roll(line, half, -1))

    def line_of(vector):
        return turn(vector.astype(F32)[None, :])

    gain_one = line_of(first_gain)
    bias_one = line_of(first_bias)
    gain_two = line_of(second_gain)
    bias_two = line_of(second_bias)
    output_shift = line_of(output_bias)
    outer_shift = line_of(outer_bias)
    query_shift = query_bias.astype(F32)[None, :]
    value_shift = value_bias.astype(F32)[None, :]
    inner_shift = inner_bias.astype(F32)[None, :]

    held = {}

    def fetch(name, weight, after=None):
        if paired:
            sent = weight if after is None else tie(weight, after)
            held[name] = (weight, mate(sent))
        else:
            full = lax.all_gather(weight, "shard", axis=0, tiled=True)
            held[name] = (full[:half], full[half:])
        return held[name][1]

    got_q = fetch("q", query_weight)
    got_k = fetch("k", key_weight)
    got_v = fetch("v", value_weight)
    fetch("o", output_weight, got_v)
    fetch("f", outer_weight, got_v)
    fetch("i", inner_weight, got_v)
    qkv = held["q"] + held["k"] + held["v"]

    frames_in = frames[:, 0]
    cotangent_in = cotangent[:, 0]
    offsets = jnp.concatenate(
        [quarter * v + jnp.arange(quarter, dtype=jnp.int32) for v in order]
    )

    def cut_own(array, m):
        return turn(lax.dynamic_slice_in_dim(array[m], order[0] * quarter, quarter, 0))

    def reduce_rows(parts):
        keep_a, keep_b, send_a, send_b = parts
        near_b = core(send_b)
        near_a = core(send_a)
        far = across((keep_b + near_b.astype(F32)).astype(BF))
        return keep_a, near_a, far

    def spread_rows(own):
        far = across(own)
        near = core(own)
        return own, far, near, core(far)

    def exchange(slabs):
        return (slabs[0],) + tuple(blocks(slabs[s], s) for s in range(1, 4))

    state = [types.SimpleNamespace() for _ in range(micros)]
    for m in range(micros):
        s = state[m]
        length = lengths[m, 0]
        s.normed, s.low = front(m, ids, frames_in, cotangent_in, gain_one, bias_one)
        s.own = cut_own(frames_in, m)
        starts = jnp.stack([(ctx_at ^ slot) * rows for slot in range(4)])
        s.mask = jnp.where(
            starts[:, None, None] + offsets[None, None, :] < length, 0.0, -1e30
        ).astype(F32)
        live = (starts < length).astype(jnp.int32)
        places = jnp.cumsum(live) - live
        listed = jnp.sum(
            jnp.where(
                (live[None, :] == 1) & (places[None, :] == jnp.arange(4)[:, None]),
                jnp.arange(4)[None, :],
                0,
            ),
            -1,
        )
        s.plan = jnp.concatenate([jnp.sum(live)[None], listed]).astype(jnp.int32)
    for m in range(micros):
        s = state[m]
        slabs = project(ids, s.normed, qkv, query_shift, value_shift)
        s.slabs = exchange(slabs)
    for m in range(micros):
        s = state[m]
        found = attend(s.plan, s.slabs, s.mask)
        s.kept, s.total = found[4:]
        s.heads = exchange(found[:4])
    for m in range(micros):
        s = state[m]
        s.mixed, *parts = output_part(ids, s.heads, held["o"])
        s.middle, low_two = middle_norm(
            *reduce_rows(parts), s.own, output_shift, gain_two, bias_two
        )
        s.spread = spread_rows(low_two)
    for m in range(micros):
        s = state[m]
        found = feed(s.spread, s.low, held["i"], held["f"], inner_shift)
        s.normed_two, s.active, s.inner, s.inner_sum = found[:4]
        s.forward = found[4:8]
        s.final_own = s.low[:quarter]
        s.keep_two = reduce_rows(found[8:])

    def weight_grad(lefts, rights):
        if paired:
            away = sum(dot_tn(a[:, half:], b) for a, b in zip(lefts, rights))
            came = mate(away.astype(BF))
            home = sum(dot_tn(a[:, :half], b) for a, b in zip(lefts, rights))
            return home, came
        full = sum(dot_tn(a, b) for a, b in zip(lefts, rights))
        return lax.psum_scatter(
            full.astype(BF), "shard", scatter_dimension=0, tiled=True
        ), None

    def joined(pair):
        home, came = pair
        return home if came is None else (home + came.astype(F32)).astype(BF)

    inner_pair = (ctx_at == 1) | (ctx_at == 2)
    hops = ([(0, 1), (3, 2)], [(1, 2), (2, 1)], [(1, 0), (2, 3)])

    def hop(stage, values):
        return [lax.ppermute(v, "ctx", hops[stage]) for v in values]

    def plus(values, others):
        return [(a.astype(F32) + b.astype(F32)).astype(BF) for a, b in zip(values, others)]

    def finish(whole, third):
        done = [jnp.where(inner_pair, a, b).astype(F32) for a, b in zip(whole, third)]
        return done[0] if len(done) == 1 else jnp.concatenate(done, 0)

    def cut(value, count):
        step = value.shape[0] // count
        return [value[i * step : (i + 1) * step] for i in range(count)]

    def tied(values, *others):
        return list(lax.optimization_barrier((tuple(values),) + others)[0])

    grads = {}
    pieces = 2 if (width // shard_count) % 32 == 0 else 1
    every = lambda name: [getattr(s, name) for s in state]
    outer = weight_grad(every("low"), every("active"))
    inner = weight_grad(every("normed_two"), every("inner"))
    for m in range(micros):
        s = state[m]
        found = middle_back(*s.keep_two, s.middle, s.final_own, gain_two)
        s.grad_middle, low_middle, s.gain_two, s.bias_two, s.shift_out = found
        s.low_parts = spread_rows(low_middle)
    outer = cut(joined(outer), pieces)
    outer_first = hop(0, outer)
    for m in range(micros):
        s = state[m]
        parts = s.low_parts if m else tied(s.low_parts, outer)
        s.low_middle, *slabs = attended_grad(ids, parts, held["o"])
        s.head_grads = exchange(slabs)
    output = weight_grad(every("low_middle"), every("mixed"))
    for m in range(micros):
        s = state[m]
        s.slabs_back = attend_back(
            s.plan, s.slabs, s.head_grads, s.kept, s.total, s.mask
        )
        s.back = exchange(s.slabs_back)
    inner = cut(joined(inner), pieces)
    output = [joined(output)]
    outer = plus(outer, outer_first)
    inner_first = hop(0, inner)
    outer_second = hop(1, outer)
    output_first = hop(0, output)
    last = micros - 1
    for m in range(micros):
        s = state[m]
        back = s.back if m != last else tied(s.back, inner, outer, output)
        found = project_back(ids, back, qkv)
        s.gq, s.gk, s.gv, s.q_sum, s.v_sum = found[:5]
        s.keep_one = reduce_rows(found[5:])
    names = "kvq"
    three = {
        n: weight_grad(every("normed"), every(g)) for n, g in zip(names, ("gk", "gv", "gq"))
    }
    for m in range(micros):
        s = state[m]
        out, s.gain_one, s.bias_one = first_back(
            *s.keep_one, s.own, s.grad_middle, gain_one
        )
        s.frames_grad = spread_rows(out)
    outer = plus(outer, outer_second)
    inner = plus(inner, inner_first)
    output = plus(output, output_first)
    outer_third = hop(2, outer)
    inner_second = hop(1, inner)
    output_second = hop(1, output)
    three = {n: tied([joined(three[n])], inner, outer, output) for n in names}
    three_first = {n: hop(0, three[n]) for n in names}
    inner = plus(inner, inner_second)
    output = plus(output, output_second)
    inner_third = hop(2, inner)
    output_third = hop(2, output)
    three = {n: plus(three[n], three_first[n]) for n in names}
    three_second = {n: hop(1, three[n]) for n in names}
    three = {n: plus(three[n], three_second[n]) for n in names}
    for n in names:
        grads[n] = finish(three[n], hop(2, three[n]))
    grads["f"] = finish(outer, outer_third)
    grads["i"] = finish(inner, inner_third)
    grads["o"] = finish(output, output_third)
    for m in range(micros):
        s = state[m]
        keep, near, far = reduce_rows(tied(s.forward, state[last].slabs_back[0]))
        final = (
            s.middle + (keep + near.astype(F32) + far.astype(F32)) + outer_shift
        ).astype(BF)
        s.result = spread_rows(final)
    result = gather_rows(ids, sum((s.result for s in state), ()))
    frames_grad = gather_rows(ids, sum((s.frames_grad for s in state), ()))

    def over_all(value):
        value = value + core(value)
        return value + across(value)

    def over_frames(value):
        value = value + mate(value) if paired else lax.psum(value, "shard")
        value = value + blocks(value, 1)
        return value + blocks(value, 2)

    def both(name):
        return sum(every(name))

    shift_final = sum(
        jnp.sum(s.final_own.astype(F32), 0, keepdims=True) for s in state
    )
    small = jnp.concatenate(
        [
            turn(both("gain_one")),
            turn(both("bias_one")),
            turn(both("gain_two")),
            turn(both("bias_two")),
            turn(both("shift_out")),
            turn(shift_final),
        ],
        0,
    )
    small = over_all(small)
    group = query_weight.shape[1]
    hidden = inner_weight.shape[1]
    narrow = jnp.concatenate([both("inner_sum"), both("q_sum"), both("v_sum")], 1)
    room = -narrow.shape[1] % width
    narrow = jnp.pad(narrow, ((0, 0), (0, room))).reshape(-1, width)
    small = over_frames(jnp.concatenate([small, narrow], 0))
    narrow = small[6:].reshape(-1)
    return (
        result,
        frames_grad,
        small[0],
        small[1],
        grads["q"],
        narrow[hidden : hidden + group],
        grads["k"],
        grads["v"],
        narrow[hidden + group : hidden + 2 * group],
        grads["o"],
        small[4],
        small[2],
        small[3],
        grads["i"],
        narrow[:hidden],
        grads["f"],
        small[5],
    )


def layer(sizes, *arrays):
    return per_device(sizes, *arrays)


def solution(mesh):
    split = P(None, "shard", "ctx", None)
    cut = P("shard", "tp")
    ins = (split, P(None, "shard"), P(), P(), cut, P("tp"), cut, cut, P("tp"), cut)
    ins += (P(), P(), P(), cut, P("tp"), cut, P(), split)
    outs = (split, split, P(), P(), cut, P("tp"), cut, cut, P("tp"), cut)
    outs += (P(), P(), P(), cut, P("tp"), cut, P())
    return jax.shard_map(
        functools.partial(layer, dict(mesh.shape)),
        mesh=mesh,
        in_specs=ins,
        out_specs=outs,
        check_vma=False,
    )
```

```python
import functools
import math
import types

import jax
import jax.numpy as jnp
from jax import lax
from jax.experimental import pallas as pl
from jax.experimental.pallas import tpu as pltpu
from jax.sharding import PartitionSpec as P


HD = 80
EXT = 96
EPS = 1e-05
BF = jnp.bfloat16
F32 = jnp.float32
SCALE = 1.0 / math.sqrt(HD)
SCALE2 = SCALE * math.log2(math.e)
SLOTS = (0, 2, 1, 3)
NT = (((1,), (1,)), ((), ()))
TN = (((0,), (0,)), ((), ()))


def sds(shape, kind):
    return jax.ShapeDtypeStruct(shape, kind)


def dot(left, right):
    return jnp.dot(left, right, preferred_element_type=F32)


def dot_nt(left, right):
    return lax.dot_general(left, right, NT, preferred_element_type=F32)


def dot_tn(left, right):
    return lax.dot_general(left, right, TN, preferred_element_type=F32)


def tie(value, *others):
    return lax.optimization_barrier((value,) + others)[0]


def normalize(values):
    center = values - jnp.mean(values, -1, keepdims=True)
    spread = jnp.mean(center * center, -1, keepdims=True)
    inverse = lax.rsqrt(spread + EPS)
    return center * inverse, inverse


def norm_back(unit, inverse, grad, gain):
    scaled = grad * gain
    first = jnp.mean(scaled, -1, keepdims=True)
    second = jnp.mean(scaled * unit, -1, keepdims=True)
    return inverse * (scaled - first - unit * second)


SMEM = pl.BlockSpec(memory_space=pltpu.SMEM)


def front_kernel(micro, ids, fa, fb, ca, cb, gain, bias, normed_o, low_o):
    half = fa.shape[-1]
    rows = fa.shape[-2]
    piece = pl.program_id(0)
    va = fa[0].astype(F32)
    vb = fb[0].astype(F32)
    count = 2 * half
    mean = (jnp.sum(va, -1, keepdims=True) + jnp.sum(vb, -1, keepdims=True)) / count
    va = va - mean
    vb = vb - mean
    spread = (jnp.sum(va * va, -1, keepdims=True) + jnp.sum(vb * vb, -1, keepdims=True)) / count
    inverse = lax.rsqrt(spread + EPS)
    normed_o[:, :half] = (va * inverse * gain[:, :half] + bias[:, :half]).astype(BF)
    normed_o[:, half:] = (vb * inverse * gain[:, half:] + bias[:, half:]).astype(BF)
    start = ids[6] * (rows * 4) + ids[piece] * rows
    valid = start + lax.broadcasted_iota(jnp.int32, (rows, 1), 0) < ids[8 + micro]
    low_o[:, :half] = jnp.where(valid, ca[0].astype(F32), 0.0).astype(BF)
    low_o[:, half:] = jnp.where(valid, cb[0].astype(F32), 0.0).astype(BF)


def front(micro, ids, frames, cotangent, gain, bias):
    rows, width = frames.shape[1:]
    quarter = rows // 4
    half = width // 2
    own = pl.BlockSpec((1, quarter, half), lambda p, ids: (micro, ids[p], ids[4]))
    other = pl.BlockSpec((1, quarter, half), lambda p, ids: (micro, ids[p], ids[5]))
    line = pl.BlockSpec((1, width), lambda p, ids: (0, 0))
    out = pl.BlockSpec((quarter, width), lambda p, ids: (p, 0))
    return pl.pallas_call(
        functools.partial(front_kernel, micro),
        out_shape=(sds((rows, width), BF), sds((rows, width), BF)),
        grid_spec=pltpu.PrefetchScalarGridSpec(
            num_scalar_prefetch=1,
            grid=(4,),
            in_specs=[own, other, own, other, line, line],
            out_specs=[out, out],
        ),
    )(ids, frames, frames, cotangent, cotangent, gain, bias)


def heads_out(ids, store, offset, outs):
    for slot in range(len(outs)):
        begin = pl.multiple_of((ids[6] ^ slot) * HD, 16)
        outs[slot][offset : offset + HD, :] = store[pl.ds(begin, HD), :]


def project_kernel(ids, normed, qa, qb, ka, kb, va, vb, q_bias, v_bias, o0, o1, o2, o3, store):
    half = qa.shape[0]
    left = normed[:, :half]
    right = normed[:, half:]
    outs = (o0, o1, o2, o3)
    for order, (first, second, shift) in enumerate(
        ((qa, qb, q_bias), (ka, kb, None), (va, vb, v_bias))
    ):
        value = dot(left, first[...]) + dot(right, second[...])
        if shift is not None:
            value = value + shift[...]
        store[...] = value.T.astype(BF)
        heads_out(ids, store, order * HD, outs)


def project(ids, normed, weights, q_bias, v_bias):
    rows = normed.shape[0]
    width = weights[0].shape[1]
    return pl.pallas_call(
        project_kernel,
        out_shape=tuple(sds((3 * HD, rows), BF) for _ in range(4)),
        in_specs=[SMEM] + [pl.BlockSpec()] * 9,
        scratch_shapes=[pltpu.VMEM((width, rows), BF)],
    )(ids, normed, *weights, q_bias, v_bias)


def attend_kernel(plan, x0, x1, x2, x3, mask, o0, o1, o2, o3, kept, total, qs, ks, vs):
    rows = x0.shape[1]
    tail = EXT - HD
    first = lax.broadcasted_iota(jnp.int32, (tail, rows), 0) == 0
    ones = jnp.where(first, 1.0, 0.0).astype(BF)
    for slot, ref in enumerate((x0, x1, x2, x3)):
        qs[slot, :HD, :] = ref[:HD, :]
        qs[slot, HD:, :] = ones
        vs[slot, :HD, :] = ref[2 * HD :, :]
        vs[slot, HD:, :] = ones
        shift = jnp.where(first, mask[slot], 0.0)
        whole = jnp.concatenate([ref[HD : 2 * HD, :].astype(F32), shift], 0)
        ks[slot] = whole.T.astype(BF)
    has = plan[0] > 0

    def query_step(i, carry):
        query = qs[i]

        def key_step(n, acc):
            j = plan[1 + n]
            score = dot(ks[j], query)
            expo = jnp.exp2(score * SCALE2).astype(BF)
            return acc + dot(vs[j], expo)

        acc = lax.fori_loop(0, plan[0], key_step, jnp.zeros((EXT, rows), F32))
        denom = jnp.where(has, acc[HD : HD + 1, :], 1.0)
        attended = acc[:HD, :] / denom
        kept[i] = attended
        total[i] = denom
        return carry

    lax.fori_loop(0, 4, query_step, 0)
    for slot, ref in enumerate((o0, o1, o2, o3)):
        ref[...] = kept[slot].astype(BF)


def attend(plan, slabs, mask):
    rows = slabs[0].shape[1]
    return pl.pallas_call(
        attend_kernel,
        out_shape=tuple(sds((HD, rows), BF) for _ in range(4))
        + (sds((4, HD, rows), F32), sds((4, 1, rows), F32)),
        in_specs=[SMEM] + [pl.BlockSpec()] * 5,
        scratch_shapes=[
            pltpu.VMEM((4, EXT, rows), BF),
            pltpu.VMEM((4, rows, EXT), BF),
            pltpu.VMEM((4, EXT, rows), BF),
        ],
    )(plan, *slabs, mask)


def attend_back_kernel(
    plan,
    x0,
    x1,
    x2,
    x3,
    g0,
    g1,
    g2,
    g3,
    kept,
    total,
    mask,
    o0,
    o1,
    o2,
    o3,
    qs,
    qt,
    ks,
    kt,
    vs,
    ss,
    st,
    deltas,
    gq,
    gk,
    gv,
):
    rows = x0.shape[1]
    tail = EXT - HD
    first = lax.broadcasted_iota(jnp.int32, (tail, rows), 0) == 0
    ones = jnp.where(first, 1.0, 0.0).astype(BF)
    blank = jnp.zeros((tail, rows), BF)
    blank_wide = jnp.zeros((tail, rows), F32)
    for slot, (ref, grad_ref) in enumerate(zip((x0, x1, x2, x3), (g0, g1, g2, g3))):
        qs[slot, :HD, :] = ref[:HD, :]
        qs[slot, HD:, :] = ones
        qt[slot] = jnp.concatenate([ref[:HD, :].astype(F32), blank_wide], 0).T.astype(BF)
        kt[slot] = ref[HD : 2 * HD, :]
        shift = jnp.where(first, mask[slot], 0.0)
        ks[slot] = jnp.concatenate([ref[HD : 2 * HD, :].astype(F32), shift], 0).T.astype(BF)
        vs[slot] = jnp.concatenate([ref[2 * HD :, :].astype(F32), blank_wide], 0).T.astype(BF)
        grad = grad_ref[...].astype(F32)
        recip = 1.0 / total[slot]
        deltas[slot] = jnp.sum(grad * kept[slot], 0, keepdims=True) * recip
        scaled = (grad * recip).astype(BF)
        ss[slot, :HD, :] = scaled
        ss[slot, HD:, :] = blank
        st[slot] = jnp.concatenate([scaled.astype(F32), blank_wide], 0).T.astype(BF)
    gq[...] = jnp.zeros_like(gq)
    gk[...] = jnp.zeros_like(gk)
    gv[...] = jnp.zeros_like(gv)

    def query_step(m, carry):
        i = plan[1 + m]

        def key_step(n, acc):
            j = plan[1 + n]
            score = dot(ks[j], qs[i])
            expo = jnp.exp2(score * SCALE2)
            through = dot(vs[j], ss[i])
            raw = (expo * (through - deltas[i])).astype(BF)
            gv[j] += dot(expo.astype(BF), st[i])
            gk[j] += dot(raw, qt[i])
            return acc + dot(kt[j], raw)

        gq[i] = lax.fori_loop(0, plan[0], key_step, jnp.zeros((HD, rows), F32))
        return carry

    lax.fori_loop(0, plan[0], query_step, 0)
    for slot, ref in enumerate((o0, o1, o2, o3)):
        ref[:HD, :] = (gq[slot] * SCALE).astype(BF)
        ref[HD : 2 * HD, :] = (gk[slot] * SCALE).T[:HD, :].astype(BF)
        ref[2 * HD :, :] = gv[slot].T[:HD, :].astype(BF)


def attend_back(plan, slabs, grads, kept, total, mask):
    rows = slabs[0].shape[1]
    return pl.pallas_call(
        attend_back_kernel,
        out_shape=tuple(sds((3 * HD, rows), BF) for _ in range(4)),
        in_specs=[SMEM] + [pl.BlockSpec()] * 11,
        scratch_shapes=[
            pltpu.VMEM((4, EXT, rows), BF),
            pltpu.VMEM((4, rows, EXT), BF),
            pltpu.VMEM((4, rows, EXT), BF),
            pltpu.VMEM((4, HD, rows), BF),
            pltpu.VMEM((4, rows, EXT), BF),
            pltpu.VMEM((4, EXT, rows), BF),
            pltpu.VMEM((4, rows, EXT), BF),
            pltpu.VMEM((4, 1, rows), F32),
            pltpu.VMEM((4, HD, rows), F32),
            pltpu.VMEM((4, rows, EXT), F32),
            pltpu.VMEM((4, rows, EXT), F32),
        ],
    )(plan, *slabs, *grads, kept, total, mask)


def split_out(left, right, half, keep_a, keep_b, send_a, send_b):
    quarter = keep_a.shape[0]
    for value, lanes in ((left, slice(0, half)), (right, slice(half, 2 * half))):
        send_b[:, lanes] = value[3 * quarter :].astype(BF)
        send_a[:, lanes] = value[2 * quarter : 3 * quarter].astype(BF)
        keep_b[:, lanes] = value[quarter : 2 * quarter]
        keep_a[:, lanes] = value[:quarter]


def parts_shape(quarter, width):
    return (
        sds((quarter, width), F32),
        sds((quarter, width), F32),
        sds((quarter, width), BF),
        sds((quarter, width), BF),
    )


def output_kernel(ids, m0, m1, m2, m3, wa, wb, mixed_o, keep_a, keep_b, send_a, send_b, store):
    for slot, ref in enumerate((m0, m1, m2, m3)):
        begin = pl.multiple_of((ids[6] ^ slot) * HD, 16)
        store[pl.ds(begin, HD), :] = ref[...]
    mixed = store[...].astype(F32).T.astype(BF)
    mixed_o[...] = mixed
    half = wa.shape[0]
    split_out(
        dot_nt(mixed, wa[...]), dot_nt(mixed, wb[...]), half, keep_a, keep_b, send_a, send_b
    )


def output_part(ids, slabs, weights):
    rows = slabs[0].shape[1]
    half, width = weights[0].shape
    return pl.pallas_call(
        output_kernel,
        out_shape=(sds((rows, width), BF),) + parts_shape(rows // 4, 2 * half),
        in_specs=[SMEM] + [pl.BlockSpec()] * 6,
        scratch_shapes=[pltpu.VMEM((width, rows), BF)],
    )(ids, *slabs, *weights)


def middle_kernel(keep, first, second, frames, shift, gain, bias, middle_o, low_o):
    middle = (
        frames[...].astype(F32)
        + (keep[...] + first[...].astype(F32) + second[...].astype(F32))
        + shift[...]
    )
    middle_o[...] = middle
    unit, _ = normalize(middle)
    low_o[...] = (unit * gain[...] + bias[...]).astype(BF)


def middle_norm(keep, first, second, frames, shift, gain, bias):
    shape = keep.shape
    return pl.pallas_call(
        middle_kernel, out_shape=(sds(shape, F32), sds(shape, BF))
    )(keep, first, second, frames, shift, gain, bias)


def feed_kernel(
    n0,
    n1,
    n2,
    n3,
    low,
    ia,
    ib,
    oa,
    ob,
    shift,
    normed_o,
    active_o,
    inner_o,
    shift_o,
    fa,
    fb,
    fc,
    fd,
    ba,
    bb,
    bc,
    bd,
    acc_f,
    acc_b,
):
    step = pl.program_id(0)
    half = ia.shape[0]
    quarter = n0.shape[0]

    @pl.when(step == 0)
    def _():
        for slot, ref in enumerate((n0, n1, n2, n3)):
            normed_o[slot * quarter : (slot + 1) * quarter, :] = ref[...]
        acc_f[...] = jnp.zeros_like(acc_f)
        acc_b[...] = jnp.zeros_like(acc_b)

    inner = dot(normed_o[:, :half], ia[...]) + dot(normed_o[:, half:], ib[...]) + shift[...]
    chance = 0.5 * (1.0 + lax.erf(inner * math.sqrt(0.5)))
    active = (inner * chance).astype(BF)
    active_o[...] = active
    slope = chance + inner * jnp.exp(-0.5 * inner * inner) * (1.0 / math.sqrt(2.0 * math.pi))
    grad = (dot(low[:, :half], oa[...]) + dot(low[:, half:], ob[...])) * slope
    shift_o[...] = jnp.sum(grad, 0, keepdims=True)
    grad_low = grad.astype(BF)
    inner_o[...] = grad_low
    acc_b[:, :half] += dot_nt(grad_low, ia[...])
    acc_b[:, half:] += dot_nt(grad_low, ib[...])
    acc_f[:, :half] += dot_nt(active, oa[...])
    acc_f[:, half:] += dot_nt(active, ob[...])

    @pl.when(step == pl.num_programs(0) - 1)
    def _():
        split_out(acc_b[:, :half], acc_b[:, half:], half, ba, bb, bc, bd)
        split_out(acc_f[:, :half], acc_f[:, half:], half, fa, fb, fc, fd)


def feed(parts, low, inner, outer, shift):
    quarter, width = parts[0].shape
    rows = 4 * quarter
    half, hidden = inner[0].shape
    block = 256
    whole = lambda *shape: pl.BlockSpec(shape, lambda f: (0,) * len(shape))
    cols = lambda count: pl.BlockSpec((count, block), lambda f: (0, f))
    part = whole(quarter, width)
    return pl.pallas_call(
        feed_kernel,
        grid=(hidden // block,),
        out_shape=(
            sds((rows, width), BF),
            sds((rows, hidden), BF),
            sds((rows, hidden), BF),
            sds((1, hidden), F32),
        )
        + parts_shape(quarter, width)
        + parts_shape(quarter, width),
        in_specs=[part] * 4 + [whole(rows, width)] + [cols(half)] * 4 + [cols(1)],
        out_specs=(whole(rows, width), cols(rows), cols(rows), cols(1)) + (part,) * 8,
        scratch_shapes=[pltpu.VMEM((rows, width), F32), pltpu.VMEM((rows, width), F32)],
    )(*parts, low, *inner, *outer, shift)


def middle_back_kernel(
    keep, first, second, middle, final, gain, grad_o, low_o, gain_o, bias_o, shift_o
):
    grad = keep[...] + first[...].astype(F32) + second[...].astype(F32)
    unit, inverse = normalize(middle[...])
    gain_o[...] = jnp.sum(grad * unit, 0, keepdims=True)
    bias_o[...] = jnp.sum(grad, 0, keepdims=True)
    total = final[...].astype(F32) + norm_back(unit, inverse, grad, gain[...])
    grad_o[...] = total
    low_o[...] = total.astype(BF)
    shift_o[...] = jnp.sum(total, 0, keepdims=True)


def middle_back(keep, first, second, middle, final, gain):
    shape = keep.shape
    line = sds((1, shape[1]), F32)
    return pl.pallas_call(
        middle_back_kernel,
        out_shape=(sds(shape, F32), sds(shape, BF), line, line, line),
    )(keep, first, second, middle, final, gain)


def attended_kernel(ids, l0, l1, l2, l3, wa, wb, low_o, o0, o1, o2, o3, store):
    half = wa.shape[0]
    quarter = l0.shape[0]
    for slot, ref in enumerate((l0, l1, l2, l3)):
        low_o[slot * quarter : (slot + 1) * quarter, :] = ref[...]
    value = dot(low_o[:, :half], wa[...]) + dot(low_o[:, half:], wb[...])
    store[...] = value.T.astype(BF)
    heads_out(ids, store, 0, (o0, o1, o2, o3))


def attended_grad(ids, parts, weights):
    quarter, width = parts[0].shape
    rows = 4 * quarter
    group = weights[0].shape[1]
    return pl.pallas_call(
        attended_kernel,
        out_shape=(sds((rows, width), BF),) + tuple(sds((HD, rows), BF) for _ in range(4)),
        in_specs=[SMEM] + [pl.BlockSpec()] * 6,
        scratch_shapes=[pltpu.VMEM((group, rows), BF)],
    )(ids, *parts, *weights)


def project_back_kernel(
    ids,
    s0,
    s1,
    s2,
    s3,
    qa,
    qb,
    ka,
    kb,
    va,
    vb,
    gq,
    gk,
    gv,
    q_sum,
    v_sum,
    keep_a,
    keep_b,
    send_a,
    send_b,
    store,
):
    half = qa.shape[0]
    left = None
    right = None
    for order, (first, second, out, total) in enumerate(
        ((qa, qb, gq, q_sum), (ka, kb, gk, None), (va, vb, gv, v_sum))
    ):
        for slot, ref in enumerate((s0, s1, s2, s3)):
            begin = pl.multiple_of((ids[6] ^ slot) * HD, 16)
            store[pl.ds(begin, HD), :] = ref[order * HD : (order + 1) * HD, :]
        wide = store[...].astype(F32).T
        grad = wide.astype(BF)
        out[...] = grad
        if total is not None:
            total[...] = jnp.sum(wide, 0, keepdims=True)
        term_left = dot_nt(grad, first[...])
        term_right = dot_nt(grad, second[...])
        left = term_left if left is None else left + term_left
        right = term_right if right is None else right + term_right
    split_out(left, right, half, keep_a, keep_b, send_a, send_b)


def project_back(ids, slabs, weights):
    rows = slabs[0].shape[1]
    half, group = weights[0].shape
    return pl.pallas_call(
        project_back_kernel,
        out_shape=tuple(sds((rows, group), BF) for _ in range(3))
        + (sds((1, group), F32), sds((1, group), F32))
        + parts_shape(rows // 4, 2 * half),
        in_specs=[SMEM] + [pl.BlockSpec()] * 10,
        scratch_shapes=[pltpu.VMEM((group, rows), BF)],
    )(ids, *slabs, *weights)


def first_back_kernel(keep, first, second, frames, middle_grad, gain, out_o, gain_o, bias_o):
    grad = keep[...] + first[...].astype(F32) + second[...].astype(F32)
    unit, inverse = normalize(frames[...].astype(F32))
    gain_o[...] = jnp.sum(grad * unit, 0, keepdims=True)
    bias_o[...] = jnp.sum(grad, 0, keepdims=True)
    out_o[...] = (middle_grad[...] + norm_back(unit, inverse, grad, gain[...])).astype(BF)


def first_back(keep, first, second, frames, middle_grad, gain):
    shape = keep.shape
    line = sds((1, shape[1]), F32)
    return pl.pallas_call(
        first_back_kernel, out_shape=(sds(shape, BF), line, line)
    )(keep, first, second, frames, middle_grad, gain)


def gather_kernel(ids, *refs):
    out = refs[-1]
    micro = pl.program_id(0)
    piece = pl.program_id(1)
    half = out.shape[-1] // 2
    for m in range(len(refs) // 4):
        for p in range(4):

            @pl.when((micro == m) & (piece == p))
            def _(ref=refs[4 * m + p]):
                left = ref[:, :half]
                right = ref[:, half:]

                @pl.when(ids[4] == 0)
                def _():
                    out[0, 0, :, :half] = left
                    out[0, 0, :, half:] = right

                @pl.when(ids[4] != 0)
                def _():
                    out[0, 0, :, :half] = right
                    out[0, 0, :, half:] = left


def gather_rows(ids, parts):
    quarter, width = parts[0].shape
    micros = len(parts) // 4
    return pl.pallas_call(
        gather_kernel,
        out_shape=sds((micros, 1, 4 * quarter, width), BF),
        grid_spec=pltpu.PrefetchScalarGridSpec(
            num_scalar_prefetch=1,
            grid=(micros, 4),
            in_specs=[pl.BlockSpec((quarter, width), lambda m, p, ids: (0, 0))] * len(parts),
            out_specs=pl.BlockSpec((1, 1, quarter, width), lambda m, p, ids: (m, 0, ids[p], 0)),
        ),
    )(ids, *parts)


def per_device(
    sizes,
    frames,
    lengths,
    first_gain,
    first_bias,
    query_weight,
    query_bias,
    key_weight,
    value_weight,
    value_bias,
    output_weight,
    output_bias,
    second_gain,
    second_bias,
    inner_weight,
    inner_bias,
    outer_weight,
    outer_bias,
    cotangent,
):
    shard_count = sizes["shard"]
    ctx_count = sizes["ctx"]
    tp_count = sizes["tp"]
    assert ctx_count == 4 and tp_count == 4
    micros = frames.shape[0]
    rows = frames.shape[2]
    width = frames.shape[3]
    half = width // 2
    quarter = rows // 4
    paired = shard_count == 2
    tp_at = lax.axis_index("tp")
    ctx_at = lax.axis_index("ctx")
    shard_at = lax.axis_index("shard") if paired else jnp.int32(0)

    def core(value):
        return lax.ppermute(value, "tp", [(i, i ^ 1) for i in range(4)])

    def across(value):
        return lax.ppermute(value, "tp", [(i, i ^ 2) for i in range(4)])

    def blocks(value, slot):
        return lax.ppermute(value, "ctx", [(i, i ^ slot) for i in range(4)])

    def mate(value):
        return lax.ppermute(value, "shard", [(0, 1), (1, 0)])

    order = [tp_at ^ slot for slot in SLOTS]
    ids = jnp.stack(
        [jnp.int32(v) for v in order]
        + [shard_at, 1 - shard_at if paired else jnp.int32(1), ctx_at, tp_at]
        + [lengths[m, 0] for m in range(micros)]
    ).astype(jnp.int32)

    def turn(line):
        if not paired:
            return line
        return jnp.where(shard_at == 0, line, jnp.roll(line, half, -1))

    def line_of(vector):
        return turn(vector.astype(F32)[None, :])

    gain_one = line_of(first_gain)
    bias_one = line_of(first_bias)
    gain_two = line_of(second_gain)
    bias_two = line_of(second_bias)
    output_shift = line_of(output_bias)
    outer_shift = line_of(outer_bias)
    query_shift = query_bias.astype(F32)[None, :]
    value_shift = value_bias.astype(F32)[None, :]
    inner_shift = inner_bias.astype(F32)[None, :]

    held = {}

    def fetch(name, weight, after=None):
        if paired:
            sent = weight if after is None else tie(weight, after)
            held[name] = (weight, mate(sent))
        else:
            full = lax.all_gather(weight, "shard", axis=0, tiled=True)
            held[name] = (full[:half], full[half:])
        return held[name][1]

    got_q = fetch("q", query_weight)
    got_k = fetch("k", key_weight)
    got_v = fetch("v", value_weight)
    fetch("o", output_weight, got_v)
    fetch("f", outer_weight, got_v)
    fetch("i", inner_weight, got_v)
    qkv = held["q"] + held["k"] + held["v"]

    frames_in = frames[:, 0]
    cotangent_in = cotangent[:, 0]
    offsets = jnp.concatenate(
        [quarter * v + jnp.arange(quarter, dtype=jnp.int32) for v in order]
    )

    def cut_own(array, m):
        return turn(lax.dynamic_slice_in_dim(array[m], order[0] * quarter, quarter, 0))

    def reduce_near(parts):
        keep_a, keep_b, send_a, send_b = parts
        near_b = core(send_b)
        near_a = core(send_a)
        return keep_a, near_a, (keep_b + near_b.astype(F32)).astype(BF)

    def reduce_far(found):
        keep_a, near_a, middle = found
        return keep_a, near_a, across(middle)

    def reduce_rows(parts):
        return reduce_far(reduce_near(parts))

    def spread_rows(own):
        far = across(own)
        near = core(own)
        return own, far, near, core(far)

    def exchange(slabs):
        return (slabs[0],) + tuple(blocks(slabs[s], s) for s in range(1, 4))

    state = [types.SimpleNamespace() for _ in range(micros)]
    for m in range(micros):
        s = state[m]
        length = lengths[m, 0]
        s.normed, s.low = front(m, ids, frames_in, cotangent_in, gain_one, bias_one)
        s.own = cut_own(frames_in, m)
        starts = jnp.stack([(ctx_at ^ slot) * rows for slot in range(4)])
        s.mask = jnp.where(
            starts[:, None, None] + offsets[None, None, :] < length, 0.0, -1e30
        ).astype(F32)
        live = (starts < length).astype(jnp.int32)
        places = jnp.cumsum(live) - live
        listed = jnp.sum(
            jnp.where(
                (live[None, :] == 1) & (places[None, :] == jnp.arange(4)[:, None]),
                jnp.arange(4)[None, :],
                0,
            ),
            -1,
        )
        s.plan = jnp.concatenate([jnp.sum(live)[None], listed]).astype(jnp.int32)
    every = lambda name: [getattr(s, name) for s in state]
    last = state[-1]

    def tied(values, *others):
        return list(lax.optimization_barrier((tuple(values),) + others)[0])

    for s, value in zip(state, tied(every("normed"))):
        s.normed = value
    previous = ()
    for m in range(micros):
        s = state[m]
        normed = tie(s.normed, *previous)
        slabs = project(ids, normed, qkv, query_shift, value_shift)
        previous = (slabs[0],)
        s.slabs = exchange(slabs)
    for m in range(micros):
        s = state[m]
        found = attend(s.plan, tied(s.slabs, *previous), s.mask)
        previous = (found[0],)
        s.kept, s.total = found[4:]
        s.heads = exchange(found[:4])
    for m in range(micros):
        s = state[m]
        s.mixed, *parts = output_part(ids, tied(s.heads, *previous), held["o"])
        previous = (s.mixed,)
        s.middle, low_two = middle_norm(
            *reduce_rows(parts), s.own, output_shift, gain_two, bias_two
        )
        s.spread = spread_rows(low_two)
    previous = ()
    for m in range(micros):
        s = state[m]
        parts = tied(s.spread, *previous)
        found = feed(parts, s.low, held["i"], held["f"], inner_shift)
        s.normed_two, s.active, s.inner, s.inner_sum = found[:4]
        s.forward = found[4:8]
        s.final_own = s.low[:quarter]
        near = reduce_near(found[8:])
        previous = (near[2],)
        s.keep_two = reduce_far(near)

    def weight_grad(lefts, rights):
        if paired:
            away = sum(dot_tn(a[:, half:], b) for a, b in zip(lefts, rights))
            came = mate(away.astype(BF))
            home = sum(dot_tn(a[:, :half], b) for a, b in zip(lefts, rights))
            return home, came
        full = sum(dot_tn(a, b) for a, b in zip(lefts, rights))
        return (
            lax.psum_scatter(full.astype(BF), "shard", scatter_dimension=0, tiled=True),
        )

    def joined(pair):
        home, came = pair if len(pair) == 2 else (pair[0], None)
        return home if came is None else (home + came.astype(F32)).astype(BF)

    inner_pair = (ctx_at == 1) | (ctx_at == 2)
    hops = ([(0, 1), (3, 2)], [(1, 2), (2, 1)], [(1, 0), (2, 3)])

    def hop(stage, values):
        return [lax.ppermute(v, "ctx", hops[stage]) for v in values]

    def plus(values, others):
        return [(a.astype(F32) + b.astype(F32)).astype(BF) for a, b in zip(values, others)]

    def finish(whole, third):
        done = [jnp.where(inner_pair, a, b).astype(F32) for a, b in zip(whole, third)]
        return done[0] if len(done) == 1 else jnp.concatenate(done, 0)

    def cut(value, count):
        step = value.shape[0] // count
        return [value[i * step : (i + 1) * step] for i in range(count)]

    grads = {}
    pieces = 2 if (width // shard_count) % 32 == 0 else 1
    previous = ()
    for m in range(micros):
        s = state[m]
        found = middle_back(
            *tied(s.keep_two, *previous), s.middle, s.final_own, gain_two
        )
        s.grad_middle, low_middle, s.gain_two, s.bias_two, s.shift_out = found
        previous = (low_middle,)
        s.low_parts = spread_rows(low_middle)
        if m == 0:
            outer = weight_grad(every("low"), every("active"))
            inner = weight_grad(every("normed_two"), every("inner"))
    previous = ()
    for m in range(micros):
        s = state[m]
        s.low_middle, *slabs = attended_grad(ids, tied(s.low_parts, *previous), held["o"])
        previous = (slabs[0],)
        s.head_grads = exchange(slabs)
    output = weight_grad(every("low_middle"), every("mixed"))
    for m in range(micros):
        s = state[m]
        s.slabs_back = attend_back(
            s.plan, s.slabs, tied(s.head_grads, *previous), s.kept, s.total, s.mask
        )
        previous = (s.slabs_back[0],)
        s.back = exchange(s.slabs_back)
    outer = cut(joined(tied(outer, *previous)), pieces)
    outer_first = hop(0, outer)
    inner = cut(joined(tied(inner, *outer)), pieces)
    inner_first = hop(0, inner)
    output = [joined(tied(output, *inner))]
    output_first = hop(0, output)
    previous = ()
    for m in range(micros):
        s = state[m]
        found = project_back(ids, tied(s.back, *previous), qkv)
        s.gq, s.gk, s.gv, s.q_sum, s.v_sum = found[:5]
        previous = (s.gq,)
        s.parts_one = found[5:]
    names = "kvq"
    three = {
        n: weight_grad(every("normed"), every(g)) for n, g in zip(names, ("gk", "gv", "gq"))
    }
    for m in range(micros):
        s = state[m]
        out, s.gain_one, s.bias_one = first_back(
            *reduce_rows(s.parts_one), s.own, s.grad_middle, gain_one
        )
        s.frames_grad = spread_rows(out)
    outer = plus(outer, outer_first)
    outer_second = hop(1, outer)
    three = {n: [joined(tied(three[n], *outer))] for n in names}
    three_first = {n: hop(0, three[n]) for n in names}
    gate = [three[n][0] for n in names]
    inner = plus(inner, tied(inner_first, *gate))
    inner_second = hop(1, inner)
    output = plus(output, tied(output_first, *gate))
    output_second = hop(1, output)
    outer = plus(outer, tied(outer_second, *inner))
    outer_third = hop(2, outer)
    three = {n: plus(three[n], tied(three_first[n], *outer)) for n in names}
    three_second = {n: hop(1, three[n]) for n in names}
    gate = [three[n][0] for n in names]
    inner = plus(inner, tied(inner_second, *gate))
    inner_third = hop(2, inner)
    output = plus(output, tied(output_second, *gate))
    output_third = hop(2, output)
    three = {n: plus(three[n], tied(three_second[n], *inner)) for n in names}
    three_third = {n: hop(2, three[n]) for n in names}
    for m in range(micros):
        s = state[m]
        keep, near, far = reduce_rows(tied(s.forward, last.slabs_back[0]))
        final = (
            s.middle + (keep + near.astype(F32) + far.astype(F32)) + outer_shift
        ).astype(BF)
        s.result = spread_rows(final)
    result = gather_rows(ids, sum((s.result for s in state), ()))
    frames_grad = gather_rows(ids, sum((s.frames_grad for s in state), ()))
    grads["f"] = finish(outer, outer_third)
    grads["i"] = finish(inner, inner_third)
    grads["o"] = finish(output, output_third)
    for n in names:
        grads[n] = finish(three[n], three_third[n])

    def over_all(value):
        value = value + core(value)
        return value + across(value)

    def over_frames(value):
        value = value + mate(value) if paired else lax.psum(value, "shard")
        value = value + blocks(value, 1)
        return value + blocks(value, 2)

    def both(name):
        return sum(every(name))

    shift_final = sum(
        jnp.sum(s.final_own.astype(F32), 0, keepdims=True) for s in state
    )
    small = jnp.concatenate(
        [
            turn(both("gain_one")),
            turn(both("bias_one")),
            turn(both("gain_two")),
            turn(both("bias_two")),
            turn(both("shift_out")),
            turn(shift_final),
        ],
        0,
    )
    small = over_all(small)
    group = query_weight.shape[1]
    hidden = inner_weight.shape[1]
    narrow = jnp.concatenate([both("inner_sum"), both("q_sum"), both("v_sum")], 1)
    room = -narrow.shape[1] % width
    narrow = jnp.pad(narrow, ((0, 0), (0, room))).reshape(-1, width)
    small = over_frames(jnp.concatenate([small, narrow], 0))
    narrow = small[6:].reshape(-1)
    return (
        result,
        frames_grad,
        small[0],
        small[1],
        grads["q"],
        narrow[hidden : hidden + group],
        grads["k"],
        grads["v"],
        narrow[hidden + group : hidden + 2 * group],
        grads["o"],
        small[4],
        small[2],
        small[3],
        grads["i"],
        narrow[:hidden],
        grads["f"],
        small[5],
    )


def layer(sizes, *arrays):
    return per_device(sizes, *arrays)


def solution(mesh):
    split = P(None, "shard", "ctx", None)
    cut = P("shard", "tp")
    ins = (split, P(None, "shard"), P(), P(), cut, P("tp"), cut, cut, P("tp"), cut)
    ins += (P(), P(), P(), cut, P("tp"), cut, P(), split)
    outs = (split, split, P(), P(), cut, P("tp"), cut, cut, P("tp"), cut)
    outs += (P(), P(), P(), cut, P("tp"), cut, P())
    return jax.shard_map(
        functools.partial(layer, dict(mesh.shape)),
        mesh=mesh,
        in_specs=ins,
        out_specs=outs,
        check_vma=False,
    )
```

```python
import functools
import math
import types

import jax
import jax.numpy as jnp
from jax import lax
from jax.experimental import pallas as pl
from jax.experimental.pallas import tpu as pltpu
from jax.sharding import PartitionSpec as P


HD = 80
EXT = 96
EPS = 1e-05
BF = jnp.bfloat16
F32 = jnp.float32
SCALE = 1.0 / math.sqrt(HD)
SCALE2 = SCALE * math.log2(math.e)
SLOTS = (0, 2, 1, 3)
NT = (((1,), (1,)), ((), ()))
TN = (((0,), (0,)), ((), ()))


def sds(shape, kind):
    return jax.ShapeDtypeStruct(shape, kind)


def dot(left, right):
    return jnp.dot(left, right, preferred_element_type=F32)


def dot_nt(left, right):
    return lax.dot_general(left, right, NT, preferred_element_type=F32)


def dot_tn(left, right):
    return lax.dot_general(left, right, TN, preferred_element_type=F32)


def tie(value, *others):
    return lax.optimization_barrier((value,) + others)[0]


def normalize(values):
    center = values - jnp.mean(values, -1, keepdims=True)
    spread = jnp.mean(center * center, -1, keepdims=True)
    inverse = lax.rsqrt(spread + EPS)
    return center * inverse, inverse


def norm_back(unit, inverse, grad, gain):
    scaled = grad * gain
    first = jnp.mean(scaled, -1, keepdims=True)
    second = jnp.mean(scaled * unit, -1, keepdims=True)
    return inverse * (scaled - first - unit * second)


SMEM = pl.BlockSpec(memory_space=pltpu.SMEM)


def front_kernel(micro, ids, fa, fb, ca, cb, gain, bias, normed_o, low_o):
    half = fa.shape[-1]
    rows = fa.shape[-2]
    piece = pl.program_id(0)
    va = fa[0].astype(F32)
    vb = fb[0].astype(F32)
    count = 2 * half
    mean = (jnp.sum(va, -1, keepdims=True) + jnp.sum(vb, -1, keepdims=True)) / count
    va = va - mean
    vb = vb - mean
    spread = (jnp.sum(va * va, -1, keepdims=True) + jnp.sum(vb * vb, -1, keepdims=True)) / count
    inverse = lax.rsqrt(spread + EPS)
    normed_o[:, :half] = (va * inverse * gain[:, :half] + bias[:, :half]).astype(BF)
    normed_o[:, half:] = (vb * inverse * gain[:, half:] + bias[:, half:]).astype(BF)
    start = ids[6] * (rows * 4) + ids[piece] * rows
    valid = start + lax.broadcasted_iota(jnp.int32, (rows, 1), 0) < ids[8 + micro]
    low_o[:, :half] = jnp.where(valid, ca[0].astype(F32), 0.0).astype(BF)
    low_o[:, half:] = jnp.where(valid, cb[0].astype(F32), 0.0).astype(BF)


def front(micro, ids, frames, cotangent, gain, bias):
    rows, width = frames.shape[1:]
    quarter = rows // 4
    half = width // 2
    own = pl.BlockSpec((1, quarter, half), lambda p, ids: (micro, ids[p], ids[4]))
    other = pl.BlockSpec((1, quarter, half), lambda p, ids: (micro, ids[p], ids[5]))
    line = pl.BlockSpec((1, width), lambda p, ids: (0, 0))
    out = pl.BlockSpec((quarter, width), lambda p, ids: (p, 0))
    return pl.pallas_call(
        functools.partial(front_kernel, micro),
        out_shape=(sds((rows, width), BF), sds((rows, width), BF)),
        grid_spec=pltpu.PrefetchScalarGridSpec(
            num_scalar_prefetch=1,
            grid=(4,),
            in_specs=[own, other, own, other, line, line],
            out_specs=[out, out],
        ),
    )(ids, frames, frames, cotangent, cotangent, gain, bias)


def heads_out(ids, store, offset, outs):
    for slot in range(len(outs)):
        begin = pl.multiple_of((ids[6] ^ slot) * HD, 16)
        outs[slot][offset : offset + HD, :] = store[pl.ds(begin, HD), :]


def project_kernel(ids, normed, qa, qb, ka, kb, va, vb, q_bias, v_bias, o0, o1, o2, o3, store):
    half = qa.shape[0]
    left = normed[:, :half]
    right = normed[:, half:]
    outs = (o0, o1, o2, o3)
    for order, (first, second, shift) in enumerate(
        ((qa, qb, q_bias), (ka, kb, None), (va, vb, v_bias))
    ):
        value = dot(left, first[...]) + dot(right, second[...])
        if shift is not None:
            value = value + shift[...]
        store[...] = value.T.astype(BF)
        heads_out(ids, store, order * HD, outs)


def project(ids, normed, weights, q_bias, v_bias):
    rows = normed.shape[0]
    width = weights[0].shape[1]
    return pl.pallas_call(
        project_kernel,
        out_shape=tuple(sds((3 * HD, rows), BF) for _ in range(4)),
        in_specs=[SMEM] + [pl.BlockSpec()] * 9,
        scratch_shapes=[pltpu.VMEM((width, rows), BF)],
    )(ids, normed, *weights, q_bias, v_bias)


def attend_kernel(plan, x0, x1, x2, x3, mask, o0, o1, o2, o3, kept, total, qs, ks, vs):
    rows = x0.shape[1]
    tail = EXT - HD
    first = lax.broadcasted_iota(jnp.int32, (tail, rows), 0) == 0
    ones = jnp.where(first, 1.0, 0.0).astype(BF)
    for slot, ref in enumerate((x0, x1, x2, x3)):
        qs[slot, :HD, :] = ref[:HD, :]
        qs[slot, HD:, :] = ones
        vs[slot, :HD, :] = ref[2 * HD :, :]
        vs[slot, HD:, :] = ones
        shift = jnp.where(first, mask[slot], 0.0)
        whole = jnp.concatenate([ref[HD : 2 * HD, :].astype(F32), shift], 0)
        ks[slot] = whole.T.astype(BF)
    has = plan[0] > 0

    def query_step(i, carry):
        query = qs[i]

        def key_step(n, acc):
            j = plan[1 + n]
            score = dot(ks[j], query)
            expo = jnp.exp2(score * SCALE2).astype(BF)
            return acc + dot(vs[j], expo)

        acc = lax.fori_loop(0, plan[0], key_step, jnp.zeros((EXT, rows), F32))
        denom = jnp.where(has, acc[HD : HD + 1, :], 1.0)
        attended = acc[:HD, :] / denom
        kept[i] = attended
        total[i] = denom
        return carry

    lax.fori_loop(0, 4, query_step, 0)
    for slot, ref in enumerate((o0, o1, o2, o3)):
        ref[...] = kept[slot].astype(BF)


def attend(plan, slabs, mask):
    rows = slabs[0].shape[1]
    return pl.pallas_call(
        attend_kernel,
        out_shape=tuple(sds((HD, rows), BF) for _ in range(4))
        + (sds((4, HD, rows), F32), sds((4, 1, rows), F32)),
        in_specs=[SMEM] + [pl.BlockSpec()] * 5,
        scratch_shapes=[
            pltpu.VMEM((4, EXT, rows), BF),
            pltpu.VMEM((4, rows, EXT), BF),
            pltpu.VMEM((4, EXT, rows), BF),
        ],
    )(plan, *slabs, mask)


def attend_back_kernel(
    plan,
    x0,
    x1,
    x2,
    x3,
    g0,
    g1,
    g2,
    g3,
    kept,
    total,
    mask,
    o0,
    o1,
    o2,
    o3,
    qs,
    qt,
    ks,
    kt,
    vs,
    ss,
    st,
    deltas,
    gq,
    gk,
    gv,
):
    rows = x0.shape[1]
    tail = EXT - HD
    first = lax.broadcasted_iota(jnp.int32, (tail, rows), 0) == 0
    ones = jnp.where(first, 1.0, 0.0).astype(BF)
    blank = jnp.zeros((tail, rows), BF)
    blank_wide = jnp.zeros((tail, rows), F32)
    for slot, (ref, grad_ref) in enumerate(zip((x0, x1, x2, x3), (g0, g1, g2, g3))):
        qs[slot, :HD, :] = ref[:HD, :]
        qs[slot, HD:, :] = ones
        qt[slot] = jnp.concatenate([ref[:HD, :].astype(F32), blank_wide], 0).T.astype(BF)
        kt[slot] = ref[HD : 2 * HD, :]
        shift = jnp.where(first, mask[slot], 0.0)
        ks[slot] = jnp.concatenate([ref[HD : 2 * HD, :].astype(F32), shift], 0).T.astype(BF)
        vs[slot] = jnp.concatenate([ref[2 * HD :, :].astype(F32), blank_wide], 0).T.astype(BF)
        grad = grad_ref[...].astype(F32)
        recip = 1.0 / total[slot]
        deltas[slot] = jnp.sum(grad * kept[slot], 0, keepdims=True) * recip
        scaled = (grad * recip).astype(BF)
        ss[slot, :HD, :] = scaled
        ss[slot, HD:, :] = blank
        st[slot] = jnp.concatenate([scaled.astype(F32), blank_wide], 0).T.astype(BF)
    gq[...] = jnp.zeros_like(gq)
    gk[...] = jnp.zeros_like(gk)
    gv[...] = jnp.zeros_like(gv)

    def query_step(m, carry):
        i = plan[1 + m]

        def key_step(n, acc):
            j = plan[1 + n]
            score = dot(ks[j], qs[i])
            expo = jnp.exp2(score * SCALE2)
            through = dot(vs[j], ss[i])
            raw = (expo * (through - deltas[i])).astype(BF)
            gv[j] += dot(expo.astype(BF), st[i])
            gk[j] += dot(raw, qt[i])
            return acc + dot(kt[j], raw)

        gq[i] = lax.fori_loop(0, plan[0], key_step, jnp.zeros((HD, rows), F32))
        return carry

    lax.fori_loop(0, plan[0], query_step, 0)
    for slot, ref in enumerate((o0, o1, o2, o3)):
        ref[:HD, :] = (gq[slot] * SCALE).astype(BF)
        ref[HD : 2 * HD, :] = (gk[slot] * SCALE).T[:HD, :].astype(BF)
        ref[2 * HD :, :] = gv[slot].T[:HD, :].astype(BF)


def attend_back(plan, slabs, grads, kept, total, mask):
    rows = slabs[0].shape[1]
    return pl.pallas_call(
        attend_back_kernel,
        out_shape=tuple(sds((3 * HD, rows), BF) for _ in range(4)),
        in_specs=[SMEM] + [pl.BlockSpec()] * 11,
        scratch_shapes=[
            pltpu.VMEM((4, EXT, rows), BF),
            pltpu.VMEM((4, rows, EXT), BF),
            pltpu.VMEM((4, rows, EXT), BF),
            pltpu.VMEM((4, HD, rows), BF),
            pltpu.VMEM((4, rows, EXT), BF),
            pltpu.VMEM((4, EXT, rows), BF),
            pltpu.VMEM((4, rows, EXT), BF),
            pltpu.VMEM((4, 1, rows), F32),
            pltpu.VMEM((4, HD, rows), F32),
            pltpu.VMEM((4, rows, EXT), F32),
            pltpu.VMEM((4, rows, EXT), F32),
        ],
    )(plan, *slabs, *grads, kept, total, mask)


def split_out(left, right, half, keep_a, keep_b, send_a, send_b):
    quarter = keep_a.shape[0]
    for value, lanes in ((left, slice(0, half)), (right, slice(half, 2 * half))):
        send_b[:, lanes] = value[3 * quarter :].astype(BF)
        send_a[:, lanes] = value[2 * quarter : 3 * quarter].astype(BF)
        keep_b[:, lanes] = value[quarter : 2 * quarter]
        keep_a[:, lanes] = value[:quarter]


def parts_shape(quarter, width):
    return (
        sds((quarter, width), F32),
        sds((quarter, width), F32),
        sds((quarter, width), BF),
        sds((quarter, width), BF),
    )


def output_kernel(ids, m0, m1, m2, m3, wa, wb, mixed_o, keep_a, keep_b, send_a, send_b, store):
    for slot, ref in enumerate((m0, m1, m2, m3)):
        begin = pl.multiple_of((ids[6] ^ slot) * HD, 16)
        store[pl.ds(begin, HD), :] = ref[...]
    mixed = store[...].astype(F32).T.astype(BF)
    mixed_o[...] = mixed
    half = wa.shape[0]
    split_out(
        dot_nt(mixed, wa[...]), dot_nt(mixed, wb[...]), half, keep_a, keep_b, send_a, send_b
    )


def output_part(ids, slabs, weights):
    rows = slabs[0].shape[1]
    half, width = weights[0].shape
    return pl.pallas_call(
        output_kernel,
        out_shape=(sds((rows, width), BF),) + parts_shape(rows // 4, 2 * half),
        in_specs=[SMEM] + [pl.BlockSpec()] * 6,
        scratch_shapes=[pltpu.VMEM((width, rows), BF)],
    )(ids, *slabs, *weights)


def middle_kernel(keep, first, second, frames, shift, gain, bias, middle_o, low_o):
    middle = (
        frames[...].astype(F32)
        + (keep[...] + first[...].astype(F32) + second[...].astype(F32))
        + shift[...]
    )
    middle_o[...] = middle
    unit, _ = normalize(middle)
    low_o[...] = (unit * gain[...] + bias[...]).astype(BF)


def middle_norm(keep, first, second, frames, shift, gain, bias):
    shape = keep.shape
    return pl.pallas_call(
        middle_kernel, out_shape=(sds(shape, F32), sds(shape, BF))
    )(keep, first, second, frames, shift, gain, bias)


def feed_kernel(
    n0,
    n1,
    n2,
    n3,
    low,
    ia,
    ib,
    oa,
    ob,
    shift,
    normed_o,
    active_o,
    inner_o,
    shift_o,
    fa,
    fb,
    fc,
    fd,
    ba,
    bb,
    bc,
    bd,
    acc_f,
    acc_b,
):
    step = pl.program_id(0)
    half = ia.shape[0]
    quarter = n0.shape[0]

    @pl.when(step == 0)
    def _():
        for slot, ref in enumerate((n0, n1, n2, n3)):
            normed_o[slot * quarter : (slot + 1) * quarter, :] = ref[...]
        acc_f[...] = jnp.zeros_like(acc_f)
        acc_b[...] = jnp.zeros_like(acc_b)

    inner = dot(normed_o[:, :half], ia[...]) + dot(normed_o[:, half:], ib[...]) + shift[...]
    chance = 0.5 * (1.0 + lax.erf(inner * math.sqrt(0.5)))
    active = (inner * chance).astype(BF)
    active_o[...] = active
    slope = chance + inner * jnp.exp(-0.5 * inner * inner) * (1.0 / math.sqrt(2.0 * math.pi))
    grad = (dot(low[:, :half], oa[...]) + dot(low[:, half:], ob[...])) * slope
    shift_o[...] = jnp.sum(grad, 0, keepdims=True)
    grad_low = grad.astype(BF)
    inner_o[...] = grad_low
    acc_b[:, :half] += dot_nt(grad_low, ia[...])
    acc_b[:, half:] += dot_nt(grad_low, ib[...])
    acc_f[:, :half] += dot_nt(active, oa[...])
    acc_f[:, half:] += dot_nt(active, ob[...])

    @pl.when(step == pl.num_programs(0) - 1)
    def _():
        split_out(acc_b[:, :half], acc_b[:, half:], half, ba, bb, bc, bd)
        split_out(acc_f[:, :half], acc_f[:, half:], half, fa, fb, fc, fd)


def feed(parts, low, inner, outer, shift):
    quarter, width = parts[0].shape
    rows = 4 * quarter
    half, hidden = inner[0].shape
    block = 256
    whole = lambda *shape: pl.BlockSpec(shape, lambda f: (0,) * len(shape))
    cols = lambda count: pl.BlockSpec((count, block), lambda f: (0, f))
    part = whole(quarter, width)
    return pl.pallas_call(
        feed_kernel,
        grid=(hidden // block,),
        out_shape=(
            sds((rows, width), BF),
            sds((rows, hidden), BF),
            sds((rows, hidden), BF),
            sds((1, hidden), F32),
        )
        + parts_shape(quarter, width)
        + parts_shape(quarter, width),
        in_specs=[part] * 4 + [whole(rows, width)] + [cols(half)] * 4 + [cols(1)],
        out_specs=(whole(rows, width), cols(rows), cols(rows), cols(1)) + (part,) * 8,
        scratch_shapes=[pltpu.VMEM((rows, width), F32), pltpu.VMEM((rows, width), F32)],
    )(*parts, low, *inner, *outer, shift)


def middle_back_kernel(
    keep, first, second, middle, final, gain, grad_o, low_o, gain_o, bias_o, shift_o
):
    grad = keep[...] + first[...].astype(F32) + second[...].astype(F32)
    unit, inverse = normalize(middle[...])
    gain_o[...] = jnp.sum(grad * unit, 0, keepdims=True)
    bias_o[...] = jnp.sum(grad, 0, keepdims=True)
    total = final[...].astype(F32) + norm_back(unit, inverse, grad, gain[...])
    grad_o[...] = total
    low_o[...] = total.astype(BF)
    shift_o[...] = jnp.sum(total, 0, keepdims=True)


def middle_back(keep, first, second, middle, final, gain):
    shape = keep.shape
    line = sds((1, shape[1]), F32)
    return pl.pallas_call(
        middle_back_kernel,
        out_shape=(sds(shape, F32), sds(shape, BF), line, line, line),
    )(keep, first, second, middle, final, gain)


def attended_kernel(ids, l0, l1, l2, l3, wa, wb, low_o, o0, o1, o2, o3, store):
    half = wa.shape[0]
    quarter = l0.shape[0]
    for slot, ref in enumerate((l0, l1, l2, l3)):
        low_o[slot * quarter : (slot + 1) * quarter, :] = ref[...]
    value = dot(low_o[:, :half], wa[...]) + dot(low_o[:, half:], wb[...])
    store[...] = value.T.astype(BF)
    heads_out(ids, store, 0, (o0, o1, o2, o3))


def attended_grad(ids, parts, weights):
    quarter, width = parts[0].shape
    rows = 4 * quarter
    group = weights[0].shape[1]
    return pl.pallas_call(
        attended_kernel,
        out_shape=(sds((rows, width), BF),) + tuple(sds((HD, rows), BF) for _ in range(4)),
        in_specs=[SMEM] + [pl.BlockSpec()] * 6,
        scratch_shapes=[pltpu.VMEM((group, rows), BF)],
    )(ids, *parts, *weights)


def project_back_kernel(
    ids,
    s0,
    s1,
    s2,
    s3,
    qa,
    qb,
    ka,
    kb,
    va,
    vb,
    gq,
    gk,
    gv,
    q_sum,
    v_sum,
    keep_a,
    keep_b,
    send_a,
    send_b,
    store,
):
    half = qa.shape[0]
    left = None
    right = None
    for order, (first, second, out, total) in enumerate(
        ((qa, qb, gq, q_sum), (ka, kb, gk, None), (va, vb, gv, v_sum))
    ):
        for slot, ref in enumerate((s0, s1, s2, s3)):
            begin = pl.multiple_of((ids[6] ^ slot) * HD, 16)
            store[pl.ds(begin, HD), :] = ref[order * HD : (order + 1) * HD, :]
        wide = store[...].astype(F32).T
        grad = wide.astype(BF)
        out[...] = grad
        if total is not None:
            total[...] = jnp.sum(wide, 0, keepdims=True)
        term_left = dot_nt(grad, first[...])
        term_right = dot_nt(grad, second[...])
        left = term_left if left is None else left + term_left
        right = term_right if right is None else right + term_right
    split_out(left, right, half, keep_a, keep_b, send_a, send_b)


def project_back(ids, slabs, weights):
    rows = slabs[0].shape[1]
    half, group = weights[0].shape
    return pl.pallas_call(
        project_back_kernel,
        out_shape=tuple(sds((rows, group), BF) for _ in range(3))
        + (sds((1, group), F32), sds((1, group), F32))
        + parts_shape(rows // 4, 2 * half),
        in_specs=[SMEM] + [pl.BlockSpec()] * 10,
        scratch_shapes=[pltpu.VMEM((group, rows), BF)],
    )(ids, *slabs, *weights)


def first_back_kernel(keep, first, second, frames, middle_grad, gain, out_o, gain_o, bias_o):
    grad = keep[...] + first[...].astype(F32) + second[...].astype(F32)
    unit, inverse = normalize(frames[...].astype(F32))
    gain_o[...] = jnp.sum(grad * unit, 0, keepdims=True)
    bias_o[...] = jnp.sum(grad, 0, keepdims=True)
    out_o[...] = (middle_grad[...] + norm_back(unit, inverse, grad, gain[...])).astype(BF)


def first_back(keep, first, second, frames, middle_grad, gain):
    shape = keep.shape
    line = sds((1, shape[1]), F32)
    return pl.pallas_call(
        first_back_kernel, out_shape=(sds(shape, BF), line, line)
    )(keep, first, second, frames, middle_grad, gain)


def gather_kernel(ids, *refs):
    out = refs[-1]
    micro = pl.program_id(0)
    piece = pl.program_id(1)
    half = out.shape[-1] // 2
    for m in range(len(refs) // 4):
        for p in range(4):

            @pl.when((micro == m) & (piece == p))
            def _(ref=refs[4 * m + p]):
                left = ref[:, :half]
                right = ref[:, half:]

                @pl.when(ids[4] == 0)
                def _():
                    out[0, 0, :, :half] = left
                    out[0, 0, :, half:] = right

                @pl.when(ids[4] != 0)
                def _():
                    out[0, 0, :, :half] = right
                    out[0, 0, :, half:] = left


def gather_rows(ids, parts):
    quarter, width = parts[0].shape
    micros = len(parts) // 4
    return pl.pallas_call(
        gather_kernel,
        out_shape=sds((micros, 1, 4 * quarter, width), BF),
        grid_spec=pltpu.PrefetchScalarGridSpec(
            num_scalar_prefetch=1,
            grid=(micros, 4),
            in_specs=[pl.BlockSpec((quarter, width), lambda m, p, ids: (0, 0))] * len(parts),
            out_specs=pl.BlockSpec((1, 1, quarter, width), lambda m, p, ids: (m, 0, ids[p], 0)),
        ),
    )(ids, *parts)


def per_device(
    sizes,
    frames,
    lengths,
    first_gain,
    first_bias,
    query_weight,
    query_bias,
    key_weight,
    value_weight,
    value_bias,
    output_weight,
    output_bias,
    second_gain,
    second_bias,
    inner_weight,
    inner_bias,
    outer_weight,
    outer_bias,
    cotangent,
):
    shard_count = sizes["shard"]
    ctx_count = sizes["ctx"]
    tp_count = sizes["tp"]
    assert ctx_count == 4 and tp_count == 4
    micros = frames.shape[0]
    rows = frames.shape[2]
    width = frames.shape[3]
    half = width // 2
    quarter = rows // 4
    paired = shard_count == 2
    tp_at = lax.axis_index("tp")
    ctx_at = lax.axis_index("ctx")
    shard_at = lax.axis_index("shard") if paired else jnp.int32(0)

    def core(value):
        return lax.ppermute(value, "tp", [(i, i ^ 1) for i in range(4)])

    def across(value):
        return lax.ppermute(value, "tp", [(i, i ^ 2) for i in range(4)])

    def blocks(value, slot):
        return lax.ppermute(value, "ctx", [(i, i ^ slot) for i in range(4)])

    def mate(value):
        return lax.ppermute(value, "shard", [(0, 1), (1, 0)])

    order = [tp_at ^ slot for slot in SLOTS]
    ids = jnp.stack(
        [jnp.int32(v) for v in order]
        + [shard_at, 1 - shard_at if paired else jnp.int32(1), ctx_at, tp_at]
        + [lengths[m, 0] for m in range(micros)]
    ).astype(jnp.int32)

    def turn(line):
        if not paired:
            return line
        return jnp.where(shard_at == 0, line, jnp.roll(line, half, -1))

    def line_of(vector):
        return turn(vector.astype(F32)[None, :])

    gain_one = line_of(first_gain)
    bias_one = line_of(first_bias)
    gain_two = line_of(second_gain)
    bias_two = line_of(second_bias)
    output_shift = line_of(output_bias)
    outer_shift = line_of(outer_bias)
    query_shift = query_bias.astype(F32)[None, :]
    value_shift = value_bias.astype(F32)[None, :]
    inner_shift = inner_bias.astype(F32)[None, :]

    held = {}

    def fetch(name, weight, after=None):
        if paired:
            sent = weight if after is None else tie(weight, after)
            held[name] = (weight, mate(sent))
        else:
            full = lax.all_gather(weight, "shard", axis=0, tiled=True)
            held[name] = (full[:half], full[half:])
        return held[name][1]

    got_q = fetch("q", query_weight)
    got_k = fetch("k", key_weight)
    got_v = fetch("v", value_weight)
    fetch("o", output_weight, got_v)
    fetch("f", outer_weight, got_v)
    fetch("i", inner_weight, got_v)
    qkv = held["q"] + held["k"] + held["v"]

    frames_in = frames[:, 0]
    cotangent_in = cotangent[:, 0]
    offsets = jnp.concatenate(
        [quarter * v + jnp.arange(quarter, dtype=jnp.int32) for v in order]
    )

    def cut_own(array, m):
        return turn(lax.dynamic_slice_in_dim(array[m], order[0] * quarter, quarter, 0))

    def reduce_near(parts):
        keep_a, keep_b, send_a, send_b = parts
        near_b = core(send_b)
        near_a = core(send_a)
        return keep_a, near_a, (keep_b + near_b.astype(F32)).astype(BF)

    def reduce_far(found):
        keep_a, near_a, middle = found
        return keep_a, near_a, across(middle)

    def reduce_rows(parts):
        return reduce_far(reduce_near(parts))

    def spread_rows(own):
        far = across(own)
        near = core(own)
        return own, far, near, core(far)

    def exchange(slabs):
        return (slabs[0],) + tuple(blocks(slabs[s], s) for s in range(1, 4))

    state = [types.SimpleNamespace() for _ in range(micros)]
    for m in range(micros):
        s = state[m]
        length = lengths[m, 0]
        s.normed, s.low = front(m, ids, frames_in, cotangent_in, gain_one, bias_one)
        s.own = cut_own(frames_in, m)
        starts = jnp.stack([(ctx_at ^ slot) * rows for slot in range(4)])
        s.mask = jnp.where(
            starts[:, None, None] + offsets[None, None, :] < length, 0.0, -1e30
        ).astype(F32)
        live = (starts < length).astype(jnp.int32)
        places = jnp.cumsum(live) - live
        listed = jnp.sum(
            jnp.where(
                (live[None, :] == 1) & (places[None, :] == jnp.arange(4)[:, None]),
                jnp.arange(4)[None, :],
                0,
            ),
            -1,
        )
        s.plan = jnp.concatenate([jnp.sum(live)[None], listed]).astype(jnp.int32)
    every = lambda name: [getattr(s, name) for s in state]

    def tied(values, *others):
        return list(lax.optimization_barrier((tuple(values),) + others)[0])

    for s, value in zip(state, tied(every("normed"))):
        s.normed = value
    previous = ()
    for m in range(micros):
        s = state[m]
        normed = tie(s.normed, *previous)
        slabs = project(ids, normed, qkv, query_shift, value_shift)
        previous = (slabs[0],)
        s.slabs = exchange(slabs)
    for m in range(micros):
        s = state[m]
        found = attend(s.plan, tied(s.slabs, *previous), s.mask)
        previous = (found[0],)
        s.kept, s.total = found[4:]
        s.heads = exchange(found[:4])
    for m in range(micros):
        s = state[m]
        s.mixed, *parts = output_part(ids, tied(s.heads, *previous), held["o"])
        previous = (s.mixed,)
        s.middle, low_two = middle_norm(
            *reduce_rows(parts), s.own, output_shift, gain_two, bias_two
        )
        s.spread = spread_rows(low_two)
    previous = ()
    for m in range(micros):
        s = state[m]
        parts = tied(s.spread, *previous)
        found = feed(parts, s.low, held["i"], held["f"], inner_shift)
        s.normed_two, s.active, s.inner, s.inner_sum = found[:4]
        s.forward = found[4:8]
        s.final_own = s.low[:quarter]
        near = reduce_near(found[8:])
        previous = (near[2],)
        s.keep_two = reduce_far(near)

    def weight_grad(lefts, rights):
        if paired:
            away = sum(dot_tn(a[:, half:], b) for a, b in zip(lefts, rights))
            came = mate(away.astype(BF))
            home = sum(dot_tn(a[:, :half], b) for a, b in zip(lefts, rights))
            return home, came
        full = sum(dot_tn(a, b) for a, b in zip(lefts, rights))
        return (
            lax.psum_scatter(full.astype(BF), "shard", scatter_dimension=0, tiled=True),
        )

    def joined(pair):
        home, came = pair if len(pair) == 2 else (pair[0], None)
        return home if came is None else (home + came.astype(F32)).astype(BF)

    inner_pair = (ctx_at == 1) | (ctx_at == 2)
    hops = ([(0, 1), (3, 2)], [(1, 2), (2, 1)], [(1, 0), (2, 3)])

    def hop(stage, values):
        return [lax.ppermute(v, "ctx", hops[stage]) for v in values]

    def plain_plus(values, others):
        return [(a.astype(F32) + b.astype(F32)).astype(BF) for a, b in zip(values, others)]

    def finish(whole, third):
        done = [jnp.where(inner_pair, a, b).astype(F32) for a, b in zip(whole, third)]
        return done[0] if len(done) == 1 else jnp.concatenate(done, 0)

    def cut(value, count):
        step = value.shape[0] // count
        return [value[i * step : (i + 1) * step] for i in range(count)]

    grads = {}
    pieces = 2 if (width // shard_count) % 32 == 0 else 1
    previous = ()
    for m in range(micros):
        s = state[m]
        found = middle_back(
            *tied(s.keep_two, *previous), s.middle, s.final_own, gain_two
        )
        s.grad_middle, low_middle, s.gain_two, s.bias_two, s.shift_out = found
        previous = (low_middle,)
        s.low_parts = spread_rows(low_middle)
        if m == 0:
            outer = weight_grad(every("low"), tied(every("active"), low_middle))
    inner = weight_grad(every("normed_two"), tied(every("inner"), *previous))
    previous = ()
    for m in range(micros):
        s = state[m]
        s.low_middle, *slabs = attended_grad(ids, tied(s.low_parts, *previous), held["o"])
        previous = (slabs[0],)
        s.head_grads = exchange(slabs)
    output = weight_grad(every("low_middle"), every("mixed"))
    for m in range(micros):
        s = state[m]
        s.slabs_back = attend_back(
            s.plan, s.slabs, tied(s.head_grads, *previous), s.kept, s.total, s.mask
        )
        previous = (s.slabs_back[0],)
        s.back = exchange(s.slabs_back)
    outer = cut(joined(tied(outer, *previous)), pieces)
    outer_first = hop(0, outer)
    inner = cut(joined(tied(inner, *outer)), pieces)
    inner_first = hop(0, inner)
    output = [joined(tied(output, *inner))]
    output_first = hop(0, output)
    previous = ()
    for m in range(micros):
        s = state[m]
        found = project_back(ids, tied(s.back, *previous), qkv)
        s.gq, s.gk, s.gv, s.q_sum, s.v_sum = found[:5]
        previous = (s.gq,)
        s.parts_one = found[5:]
    names = "kvq"
    three = {}
    for n, g in zip(names, ("gk", "gv", "gq")):
        three[n] = weight_grad(every("normed"), every(g))
    homes = [three[n][0] for n in names]
    outer = plain_plus(outer, tied(outer_first, *homes))
    outer_second = hop(1, outer)
    inner = plain_plus(inner, tied(inner_first, *outer))
    inner_second = hop(1, inner)
    output = plain_plus(output, tied(output_first, *inner))
    output_second = hop(1, output)
    token = output
    three_first = {}
    for n in names:
        three[n] = [joined(tied(three[n], *token))]
        three_first[n] = hop(0, three[n])
        token = three[n]
        if n == "k":
            outer = plain_plus(outer, tied(outer_second, *token))
            outer_third = hop(2, outer)
            token = outer
    early = token
    three_second = {}
    for n in names:
        three[n] = plain_plus(three[n], tied(three_first[n], *token))
        three_second[n] = hop(1, three[n])
        token = three[n]
    for m in range(micros):
        s = state[m]
        out, s.gain_one, s.bias_one = first_back(
            *tied(reduce_rows(s.parts_one), *token), s.own, s.grad_middle, gain_one
        )
        s.frames_grad = spread_rows(out)
    inner = plain_plus(inner, tied(inner_second, *token))
    inner_third = hop(2, inner)
    output = plain_plus(output, tied(output_second, *inner))
    output_third = hop(2, output)
    token = output
    three_third = {}
    for n in names:
        three[n] = plain_plus(three[n], tied(three_second[n], *token))
        three_third[n] = hop(2, three[n])
        token = three[n]
    for m in range(micros):
        s = state[m]
        keep, near, far = reduce_rows(tied(s.forward, *early))
        final = (
            s.middle + (keep + near.astype(F32) + far.astype(F32)) + outer_shift
        ).astype(BF)
        s.result = spread_rows(final)
    result = gather_rows(ids, tied(sum((s.result for s in state), ()), *inner))
    frames_grad = gather_rows(ids, tied(sum((s.frames_grad for s in state), ()), *output))
    grads["f"] = finish(outer, outer_third)
    grads["i"] = finish(inner, inner_third)
    grads["o"] = finish(output, output_third)
    for n in names:
        grads[n] = finish(three[n], three_third[n])

    def over_all(value):
        value = value + core(value)
        return value + across(value)

    def over_frames(value):
        value = value + mate(value) if paired else lax.psum(value, "shard")
        other = blocks(value, 1)
        value = value + other
        return value + blocks(tie(value, *token), 2)

    def both(name):
        return sum(every(name))

    shift_final = sum(
        jnp.sum(s.final_own.astype(F32), 0, keepdims=True) for s in state
    )
    small = jnp.concatenate(
        [
            turn(both("gain_one")),
            turn(both("bias_one")),
            turn(both("gain_two")),
            turn(both("bias_two")),
            turn(both("shift_out")),
            turn(shift_final),
        ],
        0,
    )
    small = over_all(small)
    group = query_weight.shape[1]
    hidden = inner_weight.shape[1]
    narrow = jnp.concatenate([both("inner_sum"), both("q_sum"), both("v_sum")], 1)
    room = -narrow.shape[1] % width
    narrow = jnp.pad(narrow, ((0, 0), (0, room))).reshape(-1, width)
    small = over_frames(jnp.concatenate([small, narrow], 0))
    narrow = small[6:].reshape(-1)
    return (
        result,
        frames_grad,
        small[0],
        small[1],
        grads["q"],
        narrow[hidden : hidden + group],
        grads["k"],
        grads["v"],
        narrow[hidden + group : hidden + 2 * group],
        grads["o"],
        small[4],
        small[2],
        small[3],
        grads["i"],
        narrow[:hidden],
        grads["f"],
        small[5],
    )


def layer(sizes, *arrays):
    return per_device(sizes, *arrays)


def solution(mesh):
    split = P(None, "shard", "ctx", None)
    cut = P("shard", "tp")
    ins = (split, P(None, "shard"), P(), P(), cut, P("tp"), cut, cut, P("tp"), cut)
    ins += (P(), P(), P(), cut, P("tp"), cut, P(), split)
    outs = (split, split, P(), P(), cut, P("tp"), cut, cut, P("tp"), cut)
    outs += (P(), P(), P(), cut, P("tp"), cut, P())
    return jax.shard_map(
        functools.partial(layer, dict(mesh.shape)),
        mesh=mesh,
        in_specs=ins,
        out_specs=outs,
        check_vma=False,
    )
```
